512 devices in a mesh: gx: 32 (over y_lo, z), gy: 16 (over x, y_hi, core).
Axes of the slice: x: 4, y: 4 (y_hi: 2, y_lo: 2; y = y_hi * 2 + y_lo), z: 16, core: 2. Of those that a mesh axis runs over, the one named last changes fastest.
Arguments:
- interior_inverse: bfloat16 [32, 16, 768, 768], P('gx', 'gy'), as said below
- coupling: bfloat16 [32, 16, 768, 1024], P('gx', 'gy'), may hold values from -1 to 1
- face_matrix: bfloat16 [32, 16, 4, 256, 256], P('gx', 'gy'), as said below
- face_modes: bfloat16 [32, 16, 256, 128], P('gx', 'gy'), may hold values from -0.125 to 0.125
- face_links: int32 [32, 16, 4], P('gx', 'gy'), may hold values from 0 to 1, as said below
- owner_map: int32 [32, 16, 128], P('gx', 'gy'), may hold values from 0 to 255
Outputs:
- deluxe: float32 [32, 16, 4, 256, 256], P('gx', 'gy')
- coarse_rows: float32 [32, 256, 128], P('gx', 'gy')
The draws below stay inside these ranges and needn't reach their ends.
Inputs may be any that keep to these rules, and one draw needn't show every extreme that they name: `interior_inverse`: each matrix symmetric positive definite. `face_matrix`: each block symmetric positive definite. `face_links`: face 0 of a subdomain equals face 1 of the subdomain before it along the grid rows, face 2 equals face 3 of the one before it along the columns; faces on the grid's outer boundary are 0.
All inputs are finite; a program needn't handle non-finite values.
Results may differ from the reference program's by a relative error of at most 0.0003.
Values sent between devices are 32-bit elements; how exact they have to be, the bound alone decides.
No kernel may reach another device: no remote copies, remote signals or barrier semaphores. Data moves between devices by JAX's collectives and lax.ppermute only.
A program may use at most 64 MiB of HBM per device.

```python
import jax
import jax.numpy as jnp
from jax import lax

NI = 768
NF = 256
FACES = 4
MODES = 32
GX = 32
GY = 16
NCG = 256


def draw_interior_inverse(key, part):
    first = jax.random.fold_in(key, 0)
    noise = jax.random.normal(first, (GX, GY, NI, NI), jnp.float32)
    matrix = jnp.eye(NI, dtype=jnp.float32) + (noise + jnp.swapaxes(noise, -1, -2)) * (0.4 / jnp.sqrt(2.0 * NI))
    return matrix.astype(jnp.bfloat16)


def draw_coupling(key, part):
    first = jax.random.fold_in(key, 0)
    spread = 1.0 / jnp.sqrt(1.0 * NI)
    noise = jnp.clip(jax.random.normal(first, (GX, GY, NI, FACES * NF), jnp.float32), -4.0, 4.0)
    return (noise * spread).astype(jnp.bfloat16)


def draw_face_matrix(key, part):
    first, second = jax.random.split(key)
    diagonal = jnp.exp(jax.random.uniform(second, (GX, GY, FACES, NF), jnp.float32, jnp.log(12.0), jnp.log(24.0)))
    noise = jax.random.normal(first, (GX, GY, FACES, NF, NF), jnp.float32)
    sym = (noise + jnp.swapaxes(noise, -1, -2)) * (0.15 / jnp.sqrt(2.0 * NF))
    return (sym + diagonal[..., :, None] * jnp.eye(NF, dtype=jnp.float32)).astype(jnp.bfloat16)


def draw_face_links(key, part):
    first, second = jax.random.split(key)
    row_ids = lax.broadcasted_iota(jnp.int32, (GX, GY), 0)
    col_ids = lax.broadcasted_iota(jnp.int32, (GX, GY), 1)
    down = (jax.random.randint(first, (GX, GY), 0, 4) > 0).astype(jnp.int32) * (row_ids < GX - 1).astype(jnp.int32)
    side = (jax.random.randint(second, (GX, GY), 0, 4) > 0).astype(jnp.int32) * (col_ids < GY - 1).astype(jnp.int32)
    north = jnp.concatenate([jnp.zeros((1, GY), jnp.int32), down[:-1]], 0)
    west = jnp.concatenate([jnp.zeros((GX, 1), jnp.int32), side[:, :-1]], 1)
    return jnp.stack([north, down, west, side], -1)


def set_ends(result, own_key, low, high):
    index_at = [jax.random.randint(jax.random.fold_in(own_key, axis), (), 0, length) for axis, length in enumerate(result.shape)]
    longest = result.shape.index(max(result.shape))
    next_to = index_at[:longest] + [(index_at[longest] + 1) % result.shape[longest]] + index_at[longest + 1:]
    return result.at[tuple(index_at)].set(low).at[tuple(next_to)].set(high)


def shard_levels(stream_key, dims, pieces, least, largest):
    def one(dim, shards_of):
        heights = jax.random.uniform(jax.random.fold_in(jax.random.fold_in(stream_key, 6), dim), (shards_of,), jnp.float32, least / len(pieces), largest / len(pieces))
        return jnp.repeat(jnp.exp(heights), dims[dim] // shards_of).reshape((-1,) + (1,) * (len(dims) - dim - 1))

    gain = one(*pieces[0])
    for cut in pieces[1:]:
        gain = gain * one(*cut)
    return gain


def bell_draw(stream_key, shape, scale, most, shards=(), held_as=jnp.bfloat16):
    factor_of = shard_levels(stream_key, shape, shards, -0.22, 0.18) if shards else 1.0
    entries = jax.random.normal(stream_key, shape, jnp.float32) * scale * factor_of
    return jnp.minimum(jnp.maximum(entries, -most), most).astype(held_as)


def setup_inputs(seed: int = 0) -> dict:
    keys = jax.random.split(jax.random.key(seed), 7)
    interior_inverse = draw_interior_inverse(jax.random.fold_in(keys[6], 71), 0)
    coupling = draw_coupling(jax.random.fold_in(keys[6], 71), 0)
    face_matrix = draw_face_matrix(jax.random.fold_in(keys[6], 71), 0)
    face_modes = bell_draw(keys[3], (GX, GY, NF, FACES * MODES), (8 * NF) ** -0.5, 0.125, ((0, 32), (1, 16)))
    face_links = draw_face_links(jax.random.fold_in(keys[6], 71), 0)
    owner_map = set_ends(jax.random.randint(keys[5], (GX, GY, FACES * MODES), 0, NCG), jax.random.fold_in(keys[5], 1), 0, NCG - 1).astype(jnp.int32)
    return dict(interior_inverse=interior_inverse, coupling=coupling, face_matrix=face_matrix, face_modes=face_modes, face_links=face_links, owner_map=owner_map)


def block_schur(items):
    inverse, coupling, faces = items
    solved = jnp.dot(inverse.astype(jnp.float32), coupling.astype(jnp.float32), preferred_element_type=jnp.float32).astype(jnp.bfloat16)
    gram_full = jnp.dot(coupling.T.astype(jnp.float32), solved.astype(jnp.float32), preferred_element_type=jnp.float32)
    schur_full = -0.5 * (gram_full + gram_full.T)
    for number in range(FACES):
        lower = number * NF
        schur_full = schur_full.at[lower:lower + NF, lower:lower + NF].add(faces[number].astype(jnp.float32))
    return schur_full

def deluxe_one(own_block, partner_block):
    factor = jnp.linalg.cholesky(own_block + partner_block)
    return jax.scipy.linalg.cho_solve((factor, True), own_block)

def coarse_one(items):
    schur_full, deluxe_set, modes, links = items
    phi_full = jnp.zeros((FACES * NF, FACES * MODES), schur_full.dtype)
    for number in range(FACES):
        mapped = jnp.dot(deluxe_set[number], modes[:, number * MODES:(number + 1) * MODES].astype(schur_full.dtype), precision=lax.Precision.HIGHEST)
        phi_full = phi_full.at[number * NF:(number + 1) * NF, number * MODES:(number + 1) * MODES].set(mapped)
    product = jnp.dot(schur_full, phi_full, precision=lax.Precision.HIGHEST)
    local = jnp.dot(phi_full.T, product, precision=lax.Precision.HIGHEST)
    weights = jnp.repeat(links.astype(schur_full.dtype), MODES)
    return local * weights[:, None] * weights[None, :]

def reference(interior_inverse, coupling, face_matrix, face_modes, face_links, owner_map):
    count = GX * GY
    flat = (interior_inverse.reshape(count, NI, NI), coupling.reshape(count, NI, FACES * NF), face_matrix.reshape(count, FACES, NF, NF))
    schur_all = lax.map(block_schur, flat)
    blocks = jnp.stack([schur_all[:, n * NF:(n + 1) * NF, n * NF:(n + 1) * NF] for n in range(FACES)], axis=1)
    blocks = blocks.reshape(GX, GY, FACES, NF, NF)
    zero_row = jnp.zeros((1, GY, NF, NF), blocks.dtype)
    zero_col = jnp.zeros((GX, 1, NF, NF), blocks.dtype)
    north = jnp.concatenate([zero_row, blocks[:-1, :, 1]], 0)
    south = jnp.concatenate([blocks[1:, :, 0], zero_row], 0)
    west = jnp.concatenate([zero_col, blocks[:, :-1, 3]], 1)
    east = jnp.concatenate([blocks[:, 1:, 2], zero_col], 1)
    partners = jnp.stack([north, south, west, east], 2) * face_links.astype(blocks.dtype)[..., None, None]
    deluxe = jax.vmap(deluxe_one)(blocks.reshape(-1, NF, NF), partners.reshape(-1, NF, NF)).reshape(GX, GY, FACES, NF, NF)
    local = lax.map(coarse_one, (schur_all, deluxe.reshape(count, FACES, NF, NF), face_modes.reshape(count, NF, FACES * MODES), face_links.reshape(count, FACES)))
    local = local.reshape(GX, GY, FACES * MODES, FACES * MODES)
    onehot = (owner_map[:, :, None, :] == jnp.arange(NCG, dtype=jnp.int32)[:, None]).astype(local.dtype)
    coarse_rows = jnp.einsum('ijga,ijab->igb', onehot, local, precision=lax.Precision.HIGHEST)
    return (deluxe, coarse_rows)
```

```python
import functools

import jax
import jax.numpy as jnp
from jax import lax
from jax.experimental import pallas as pl
from jax.experimental.pallas import tpu as pltpu
from jax.sharding import PartitionSpec as P

NI = 768
NF = 256
FACES = 4
MODES = 32
NCG = 256

F32 = jnp.float32
BF16 = jnp.bfloat16
NORTH, SOUTH, WEST, EAST = range(FACES)

SWEEP_TOL = 3e-4
RESIDUAL_TOL = 4e-10
MAX_SQUARINGS = 40
MAX_SWEEPS = 12


def dot(left, right):
    return lax.dot_general(left, right, (((1,), (0,)), ((), ())), preferred_element_type=F32)


def dot_rows(left, right):
    return lax.dot_general(left, right, (((0,), (0,)), ((), ())), preferred_element_type=F32)


def split(value):
    high = value.astype(BF16)
    return high, (value - high.astype(F32)).astype(BF16)


def left_three(value):
    high, low = split(value)
    return jnp.concatenate([high, high, low], axis=1)


def right_three(value):
    high, low = split(value)
    return jnp.concatenate([high, low, high], axis=0)


def odd_column():
    return lax.rem(lax.axis_index("gy"), 2) == 1


def own_kernel(first, by_column, inverse, couple, faces, solved, one, two):
    lower = first * NF
    solved[...] = dot(inverse[...], couple[:, lower : lower + 2 * NF]).astype(BF16)
    blocks = []
    for n in range(2):
        columns = slice(n * NF, (n + 1) * NF)
        gram = dot_rows(couple[:, lower + n * NF : lower + (n + 1) * NF], solved[:, columns])
        blocks.append(faces[first + n].astype(F32) - 0.5 * (gram + gram.T))
    if by_column:
        odd = odd_column()
        one[...] = jnp.where(odd, blocks[1], blocks[0])
        two[...] = jnp.where(odd, blocks[0], blocks[1])
    else:
        one[...], two[...] = blocks


def own_blocks(inverse, couple, faces, first, by_column):
    vmem = pl.BlockSpec(memory_space=pltpu.VMEM)
    block = jax.ShapeDtypeStruct((NF, NF), F32)
    return pl.pallas_call(
        functools.partial(own_kernel, first, by_column),
        out_shape=(jax.ShapeDtypeStruct((NI, 2 * NF), BF16), block, block),
        in_specs=[vmem] * 3,
        out_specs=(vmem,) * 3,
        compiler_params=pltpu.CompilerParams(vmem_limit_bytes=16 << 20),
        cost_estimate=pl.CostEstimate(
            flops=4 * NI * NI * NF + 4 * NI * NF * NF,
            bytes_accessed=2 * NI * NI + 8 * NI * NF + 12 * NF * NF,
            transcendentals=0,
        ),
        name=f"own_blocks_{first}",
    )(inverse, couple, faces)


def eye():
    rows = lax.broadcasted_iota(jnp.int32, (NF, NF), 0)
    columns = lax.broadcasted_iota(jnp.int32, (NF, NF), 1)
    return rows == columns


def coarse_kernel(
    links, sent_north, sent_south, sent_far, sent_near, north, south, far, near,
    modes, couple, solved_ns, solved_we, faces, owners,
    deluxe, partial,
    own, matrix, power, sweep, rest, scale, phi, left, right,
):
    solved = [solved_ns, solved_ns, solved_we, solved_we]
    weight = [links[n].astype(F32) for n in range(FACES)]

    odd = odd_column()
    own[NORTH] = sent_north[...]
    own[SOUTH] = sent_south[...]
    own[WEST] = jnp.where(odd, sent_near[...], sent_far[...])
    own[EAST] = jnp.where(odd, sent_far[...], sent_near[...])

    def partner(n):
        if n in (NORTH, SOUTH):
            return (north, south)[n][...]
        if n == WEST:
            return jnp.where(odd, near[...], far[...])
        return jnp.where(odd, far[...], near[...])

    own_norm = []
    for n in range(FACES):
        m = own[n] + partner(n) * weight[n]
        diagonal = jnp.sum(jnp.where(eye(), m, 0.0), axis=1, keepdims=True)
        inverse_diagonal = 1.0 / diagonal
        bound = jnp.max(jnp.sum(jnp.abs(m), axis=1, keepdims=True) * inverse_diagonal)
        factor = jnp.where(bound < 1.75, 1.0, 1.0 / bound)
        matrix[n] = m
        scale[n] = jnp.broadcast_to(inverse_diagonal * factor, (NF, 128))
        block = own[n]
        rest[n] = block
        deluxe[n] = jnp.zeros((NF, NF), F32)
        own_norm.append(jnp.sum(block * block))

    def scaled(n):
        return jnp.concatenate([scale[n]] * 2, axis=1)

    def largest(values):
        result = values[0]
        for value in values[1:]:
            result = jnp.maximum(result, value)
        return result

    def sweep_once(state):
        count, _, now = state
        norms = []
        for n in range(FACES):
            by = scaled(n)
            first = jnp.where(eye(), 1.0, 0.0) - by * matrix[n]
            start = by * rest[n]
            both = dot(left_three(first), right_three(jnp.concatenate([first, start], axis=1)))
            square = both[:, :NF]
            power[n] = square
            sweep[n] = start + both[:, NF:]
            norms.append(jnp.sum(square * square))

        def more(inner):
            return jnp.logical_and(inner[1] > SWEEP_TOL, inner[0] < MAX_SQUARINGS)

        def squaring(inner):
            found = []
            for n in range(FACES):
                error = power[n]
                start = sweep[n]
                both = dot(left_three(error), right_three(jnp.concatenate([error, start], axis=1)))
                square = both[:, :NF]
                power[n] = square
                sweep[n] = start + both[:, NF:]
                found.append(jnp.sum(square * square))
            return inner[0] + 1, largest(found)

        lax.while_loop(more, squaring, (jnp.int32(0), largest(norms)))

        ratios = []
        for n in range(FACES):
            start = sweep[n]
            total = deluxe[n] + (start + dot(left_three(power[n]), right_three(start)))
            deluxe[n] = total
            residual = own[n] - dot(left_three(matrix[n]), right_three(total))
            rest[n] = residual
            ratios.append(jnp.sum(residual * residual) / own_norm[n])
        return count + 1, now, largest(ratios)

    def unsolved(state):
        count, before, now = state
        return jnp.logical_and(
            jnp.logical_and(now > RESIDUAL_TOL, now < 0.25 * before), count < MAX_SWEEPS
        )

    lax.while_loop(unsolved, sweep_once, (jnp.int32(0), jnp.float32(8.0), jnp.float32(1.0)))

    for n in range(FACES):
        high, low = split(deluxe[n])
        mode = modes[:, n * MODES : (n + 1) * MODES]
        phi[n] = dot(high, mode) + dot(low, mode)

    local = jnp.zeros((FACES * MODES, FACES * MODES), F32)
    rows = lax.broadcasted_iota(jnp.int32, (FACES * MODES, FACES * MODES), 0)
    columns = lax.broadcasted_iota(jnp.int32, (FACES * MODES, FACES * MODES), 1)
    pieces = []
    for n in range(FACES):
        both = jnp.concatenate(split(phi[n]), axis=1)
        lower = n * NF
        one = dot(couple[:, lower : lower + NF], both)
        two = dot(solved[n][:, lower % (2 * NF) : lower % (2 * NF) + NF], both)
        three = dot(faces[n], both)
        here = slice(n * MODES, (n + 1) * MODES)
        left[:, here] = one[:, :MODES] + one[:, MODES:]
        right[:, here] = two[:, :MODES] + two[:, MODES:]
        pieces.append(three[:, :MODES] + three[:, MODES:])
    own_part = dot_three_rows(
        jnp.concatenate([phi[n] for n in range(FACES)], axis=1), jnp.concatenate(pieces, axis=1), True
    )
    cross = dot_three_rows(left[...], right[...], False)
    same = (rows // MODES) == (columns // MODES)
    local = jnp.where(same, own_part, 0.0) - 0.5 * (cross + cross.T)

    def spread(index):
        face = index // MODES
        value = jnp.zeros(index.shape, F32)
        for n in range(FACES):
            value = jnp.where(face == n, weight[n], value)
        return value

    local = local * spread(rows) * spread(columns)
    slots = lax.broadcasted_iota(jnp.int32, (NCG, FACES * MODES), 0)
    onehot = jnp.where(owners[...] == slots, 1.0, 0.0).astype(BF16)
    high, low = split(local)
    lowest = (local - high.astype(F32) - low.astype(F32)).astype(BF16)
    partial[...] = dot(onehot, high) + (dot(onehot, low) + dot(onehot, lowest))


def dot_three_rows(one, two, blocks):
    one_high, one_low = split(one)
    two_high, two_low = split(two)
    return dot_rows(one_high, two_high) + (dot_rows(one_high, two_low) + dot_rows(one_low, two_high))


def coarse_partial(links, sent, received, modes, couple, solved_ns, solved_we, faces, owners):
    vmem = pl.BlockSpec(memory_space=pltpu.VMEM)
    smem = pl.BlockSpec(memory_space=pltpu.SMEM)
    return pl.pallas_call(
        coarse_kernel,
        out_shape=(
            jax.ShapeDtypeStruct((FACES, NF, NF), F32),
            jax.ShapeDtypeStruct((NCG, FACES * MODES), F32),
        ),
        in_specs=[smem] + [vmem] * 14,
        out_specs=(vmem, vmem),
        scratch_shapes=[pltpu.VMEM((FACES, NF, NF), F32)] * 5
        + [
            pltpu.VMEM((FACES, NF, 128), F32),
            pltpu.VMEM((FACES, NF, MODES), F32),
            pltpu.VMEM((NI, FACES * MODES), F32),
            pltpu.VMEM((NI, FACES * MODES), F32),
        ],
        compiler_params=pltpu.CompilerParams(vmem_limit_bytes=28 << 20),
        cost_estimate=pl.CostEstimate(flops=8 << 30, bytes_accessed=4 << 20, transcendentals=0),
        name="coarse_partial",
    )(links, *sent, *received, modes, couple, solved_ns, solved_we, faces, owners)


def swap_pairs(value, axis, first):
    count = lax.axis_size(axis)
    pairs = []
    for low in range(first, count - 1, 2):
        pairs += [(low, low + 1), (low + 1, low)]
    return lax.ppermute(value, axis, pairs)


def shifted(value, axis, steps):
    count = lax.axis_size(axis)
    initial, last = (max(0, -steps), min(count, count - steps))
    return lax.ppermute(value, axis, [(source, source + steps) for source in range(initial, last)])


def body(interior_inverse, coupling, face_matrix, face_modes, face_links, owner_map):
    inverse = interior_inverse[0, 0]
    couple = coupling[0, 0]
    faces = face_matrix[0, 0]
    modes = face_modes[0, 0]
    links = face_links[0, 0]
    owners = owner_map[0]
    solved_we, far, near = own_blocks(inverse, couple, faces, WEST, True)
    far_part = swap_pairs(far, "gy", 1)
    solved_ns, north, south = own_blocks(inverse, couple, faces, NORTH, False)
    north_part = shifted(south, "gx", 1)
    south_part = shifted(north, "gx", -1)
    near_part = swap_pairs(near, "gy", 0)
    deluxe, partial = coarse_partial(
        links, (north, south, far, near), (north_part, south_part, far_part, near_part),
        modes, couple, solved_ns, solved_we, faces, owners,
    )
    count = lax.axis_size("gy")
    parts = partial.reshape(count, NCG // count, FACES * MODES)
    coarse = lax.all_to_all(parts, "gy", 0, 0).sum(0)
    return deluxe[None, None], coarse[None]


def solution(mesh):
    placed = (
        P("gx", "gy", None, None),
        P("gx", "gy", None, None),
        P("gx", "gy", None, None, None),
        P("gx", "gy", None, None),
        P("gx", "gy", None),
        P("gx", "gy", None),
    )
    return jax.shard_map(
        body,
        mesh=mesh,
        in_specs=placed,
        out_specs=(P("gx", "gy", None, None, None), P("gx", "gy", None)),
        check_vma=False,
    )
```

```python
import functools

import jax
import jax.numpy as jnp
from jax import lax
from jax.experimental import pallas as pl
from jax.experimental.pallas import tpu as pltpu
from jax.sharding import PartitionSpec as P

NI = 768
NF = 256
FACES = 4
MODES = 32
NCG = 256
HALF = NF // 2

F32 = jnp.float32
BF16 = jnp.bfloat16
NORTH, SOUTH, WEST, EAST = range(FACES)

SWEEP_TOL = 3e-4
RESIDUAL_TOL = 4e-10
BOUND = 2e-5
MAX_SQUARINGS = 40
MAX_SWEEPS = 12


def dot(left, right):
    return lax.dot_general(left, right, (((1,), (0,)), ((), ())), preferred_element_type=F32)


def dot_rows(left, right):
    return lax.dot_general(left, right, (((0,), (0,)), ((), ())), preferred_element_type=F32)


def split(value):
    high = value.astype(BF16)
    return high, (value - high.astype(F32)).astype(BF16)


def left_three(value):
    high, low = split(value)
    return jnp.concatenate([high, high, low], axis=1)


def right_three(value):
    high, low = split(value)
    return jnp.concatenate([high, low, high], axis=0)


def odd_column():
    return lax.rem(lax.axis_index("gy"), 2) == 1


def grid_iota(rows, columns, dimension):
    return lax.broadcasted_iota(jnp.int32, (rows, columns), dimension)


def pack(block):
    first, last = block[:HALF, :HALF], block[HALF:, HALF:]
    rows, columns = grid_iota(HALF, HALF, 0), grid_iota(HALF, HALF, 1)
    diagonal = jnp.sum(jnp.where(rows == columns, last, 0.0), axis=0, keepdims=True)
    square = jnp.where(rows >= columns, first, last)
    return square, block[:HALF, HALF:], jnp.broadcast_to(diagonal, (8, HALF))


def unpack(packed):
    square, corner, diagonal = packed[:HALF], packed[HALF:NF], packed[NF : NF + 1]
    rows, columns = grid_iota(HALF, HALF, 0), grid_iota(HALF, HALF, 1)
    turned = square.T
    first = jnp.where(rows >= columns, square, turned)
    last = jnp.where(rows == columns, diagonal, jnp.where(rows < columns, square, turned))
    return first, corner, corner.T, last


def own_kernel(
    inverse_hbm, couple_hbm, faces_hbm,
    solved, own, send_north, send_south, send_far, send_near,
    inverse, couple, faces, sems,
):
    third, half = NI // 3, 2 * NF
    copies = [
        pltpu.make_async_copy(couple_hbm.at[:, half:], couple.at[:, half:], sems.at[0]),
        *(
            pltpu.make_async_copy(
                inverse_hbm.at[pl.ds(n * third, third)], inverse.at[pl.ds(n * third, third)], sems.at[1 + n]
            )
            for n in range(3)
        ),
        pltpu.make_async_copy(faces_hbm, faces, sems.at[4]),
        pltpu.make_async_copy(couple_hbm.at[:, :half], couple.at[:, :half], sems.at[5]),
    ]
    for copy in copies:
        copy.start()
    copies[0].wait()
    for n in range(3):
        copies[1 + n].wait()
        rows = slice(n * third, (n + 1) * third)
        solved[rows, half:] = dot(inverse[rows, :], couple[:, half:]).astype(BF16)
    copies[4].wait()

    def own_of(n):
        columns = slice(n * NF, (n + 1) * NF)
        gram = dot_rows(couple[:, columns], solved[:, columns])
        block = faces[n].astype(F32) - 0.5 * (gram + gram.T)
        own[n] = block
        return pack(block)

    def put(ref, parts):
        ref[:HALF], ref[HALF:NF], ref[NF:] = parts

    odd = odd_column()
    west, east = own_of(WEST), own_of(EAST)
    put(send_far, [jnp.where(odd, e, w) for w, e in zip(west, east, strict=True)])
    put(send_near, [jnp.where(odd, w, e) for w, e in zip(west, east, strict=True)])
    copies[5].wait()
    solved[:, :half] = dot(inverse[...], couple[:, :half]).astype(BF16)
    put(send_north, own_of(NORTH))
    put(send_south, own_of(SOUTH))


def own_blocks(inverse, couple, faces):
    vmem = pl.BlockSpec(memory_space=pltpu.VMEM)
    hbm = pl.BlockSpec(memory_space=pltpu.HBM)
    send = jax.ShapeDtypeStruct((NF + 8, HALF), F32)
    return pl.pallas_call(
        own_kernel,
        out_shape=(
            jax.ShapeDtypeStruct((NI, FACES * NF), BF16),
            jax.ShapeDtypeStruct((FACES, NF, NF), F32),
            send, send, send, send,
        ),
        in_specs=[hbm] * 3,
        out_specs=(vmem,) * 6,
        scratch_shapes=[
            pltpu.VMEM((NI, NI), BF16),
            pltpu.VMEM((NI, FACES * NF), BF16),
            pltpu.VMEM((FACES, NF, NF), BF16),
            pltpu.SemaphoreType.DMA((6,)),
        ],
        compiler_params=pltpu.CompilerParams(vmem_limit_bytes=20 << 20),
        name="own_blocks",
    )(*(pltpu.with_memory_space_constraint(value, pltpu.HBM) for value in (inverse, couple, faces)))


def eye():
    rows = lax.broadcasted_iota(jnp.int32, (NF, NF), 0)
    columns = lax.broadcasted_iota(jnp.int32, (NF, NF), 1)
    return rows == columns


def largest(values):
    result = values[0]
    for value in values[1:]:
        result = jnp.maximum(result, value)
    return result


def total_square(value):
    rows = jnp.sum(value * value, axis=0, keepdims=True)
    return jnp.sum(rows, axis=1, keepdims=True)


def general_solve(own, deluxe, matrix, scale, sweep, rest, power):
    own_norm = []
    for n in range(FACES):
        m, block = matrix[n], own[n]
        by = 1.0 / jnp.sum(jnp.where(eye(), m, 0.0), axis=1, keepdims=True)
        bound = jnp.max(jnp.sum(jnp.abs(m), axis=1, keepdims=True) * by)
        factor = jnp.where(bound < 1.75, 1.0, 1.0 / bound)
        scale[n] = jnp.broadcast_to(by * factor, (NF, HALF))
        rest[n] = block
        deluxe[n] = jnp.zeros((NF, NF), F32)
        own_norm.append(jnp.sum(block * block))

    def sweep_once(state):
        count, _, now = state
        for n in range(FACES):
            by = jnp.concatenate([scale[n]] * 2, axis=1)
            power[n] = jnp.where(eye(), 1.0, 0.0) - by * matrix[n]
            sweep[n] = by * rest[n]

        def more(inner):
            return jnp.logical_and(inner[1] > SWEEP_TOL, inner[0] < MAX_SQUARINGS)

        def squaring(inner):
            found = []
            for n in range(FACES):
                error = power[n]
                start = sweep[n]
                both = dot(left_three(error), right_three(jnp.concatenate([error, start], axis=1)))
                square = both[:, :NF]
                power[n] = square
                sweep[n] = start + both[:, NF:]
                found.append(jnp.sum(square * square))
            return inner[0] + 1, largest(found)

        lax.while_loop(more, squaring, (jnp.int32(0), jnp.float32(1.0)))

        ratios = []
        for n in range(FACES):
            start = sweep[n]
            total = deluxe[n] + (start + dot(left_three(power[n]), right_three(start)))
            deluxe[n] = total
            residual = own[n] - dot(left_three(matrix[n]), right_three(total))
            rest[n] = residual
            ratios.append(jnp.sum(residual * residual) / own_norm[n])
        return count + 1, now, largest(ratios)

    def unsolved(state):
        count, before, now = state
        return jnp.logical_and(
            jnp.logical_and(now > RESIDUAL_TOL, now < 0.25 * before), count < MAX_SWEEPS
        )

    lax.while_loop(unsolved, sweep_once, (jnp.int32(0), jnp.float32(8.0), jnp.float32(1.0)))


def coarse_kernel(
    links, own, north, south, far, near, modes, couple, solved, faces, owners,
    deluxe, partial,
    matrix, scale, power, sweep, rest, phi, left, right,
):
    weight = [links[n].astype(F32) for n in range(FACES)]
    odd = odd_column()
    packed = [
        north[...],
        south[...],
        jnp.where(odd, near[...], far[...]),
        jnp.where(odd, far[...], near[...]),
    ]
    for n in range(FACES):
        quarters = unpack(packed[n])
        for at, quarter in enumerate(quarters):
            here = (slice((at // 2) * HALF, (at // 2 + 1) * HALF), slice((at % 2) * HALF, (at % 2 + 1) * HALF))
            matrix[(n, *here)] = own[(n, *here)] + quarter * weight[n]

    def inverse_diagonal(n):
        return 1.0 / jnp.sum(jnp.where(eye(), matrix[n], 0.0), axis=1, keepdims=True)

    norms = [[] for _ in range(FACES)]
    for n in range(FACES):
        by = inverse_diagonal(n)
        scale[n] = jnp.broadcast_to(by, (NF, HALF))
        first = jnp.where(eye(), 0.0, -by * matrix[n])
        norms[n].append(total_square(first))
        start = by * own[n]
        power[0, n] = first.astype(BF16)
        both = dot(power[0, n], jnp.concatenate([power[0, n], start.astype(BF16)], axis=1))
        square = both[:, :NF]
        norms[n].append(total_square(square))
        power[1, n] = square.astype(BF16)
        sweep[n] = start + both[:, NF:]
    for n in range(FACES):
        start = sweep[n]
        rounded = (start + dot(power[1, n], start.astype(BF16))).astype(BF16)
        high, low = split(matrix[n])
        residual = own[n] - (dot(high, rounded) + dot(low, rounded))
        rest[n] = jnp.concatenate([scale[n]] * 2, axis=1) * residual
        rounded = rounded.astype(F32)
        norms[n].append(total_square(rounded))
        deluxe[n] = rounded
    for n in range(FACES):
        start = rest[n]
        sweep[n] = start + dot(power[0, n], start.astype(BF16))
    left_out = []
    for n in range(FACES):
        start = sweep[n]
        step = start + dot(power[1, n], start.astype(BF16))
        deluxe[n] = deluxe[n] + step
        first, square, size = (jnp.sqrt(norm) for norm in norms[n])
        rate = norms[n][1] + (first + square) * (1.0 + first) * 2.0**-8
        left_out.append(rate * jnp.sqrt(total_square(step)) / size)
    worst = largest(left_out)

    @pl.when(jnp.logical_not(jnp.max(worst) < BOUND))
    def _():
        general_solve(own, deluxe, matrix, scale, sweep, rest, phi)

    for n in range(FACES):
        high, low = split(deluxe[n])
        mode = modes[:, n * MODES : (n + 1) * MODES]
        phi[n, :, :MODES] = dot(high, mode) + dot(low, mode)

    local = jnp.zeros((FACES * MODES, FACES * MODES), F32)
    rows = lax.broadcasted_iota(jnp.int32, (FACES * MODES, FACES * MODES), 0)
    columns = lax.broadcasted_iota(jnp.int32, (FACES * MODES, FACES * MODES), 1)
    pieces = []
    for n in range(FACES):
        both = jnp.concatenate(split(phi[n, :, :MODES]), axis=1)
        lower = n * NF
        one = dot(couple[:, lower : lower + NF], both)
        two = dot(solved[:, lower : lower + NF], both)
        three = dot(faces[n], both)
        here = slice(n * MODES, (n + 1) * MODES)
        left[:, here] = one[:, :MODES] + one[:, MODES:]
        right[:, here] = two[:, :MODES] + two[:, MODES:]
        pieces.append(three[:, :MODES] + three[:, MODES:])
    own_part = dot_three_rows(
        jnp.concatenate([phi[n, :, :MODES] for n in range(FACES)], axis=1), jnp.concatenate(pieces, axis=1), True
    )
    cross = dot_three_rows(left[...], right[...], False)
    same = (rows // MODES) == (columns // MODES)
    local = jnp.where(same, own_part, 0.0) - 0.5 * (cross + cross.T)

    def spread(index):
        face = index // MODES
        value = jnp.zeros(index.shape, F32)
        for n in range(FACES):
            value = jnp.where(face == n, weight[n], value)
        return value

    local = local * spread(rows) * spread(columns)
    slots = lax.broadcasted_iota(jnp.int32, (NCG, FACES * MODES), 0)
    onehot = jnp.where(owners[...] == slots, 1.0, 0.0).astype(BF16)
    high, low = split(local)
    lowest = (local - high.astype(F32) - low.astype(F32)).astype(BF16)
    partial[...] = dot(onehot, high) + (dot(onehot, low) + dot(onehot, lowest))


def dot_three_rows(one, two, blocks):
    one_high, one_low = split(one)
    two_high, two_low = split(two)
    return dot_rows(one_high, two_high) + (dot_rows(one_high, two_low) + dot_rows(one_low, two_high))


def coarse_partial(links, own, received, modes, couple, solved, faces, owners):
    vmem = pl.BlockSpec(memory_space=pltpu.VMEM)
    smem = pl.BlockSpec(memory_space=pltpu.SMEM)
    return pl.pallas_call(
        coarse_kernel,
        out_shape=(
            jax.ShapeDtypeStruct((FACES, NF, NF), F32),
            jax.ShapeDtypeStruct((NCG, FACES * MODES), F32),
        ),
        in_specs=[smem] + [vmem] * 10,
        out_specs=(vmem, vmem),
        scratch_shapes=[
            pltpu.VMEM((FACES, NF, NF), F32),
            pltpu.VMEM((FACES, NF, HALF), F32),
            pltpu.VMEM((2, FACES, NF, NF), BF16),
            pltpu.VMEM((FACES, NF, NF), F32),
            pltpu.VMEM((FACES, NF, NF), F32),
            pltpu.VMEM((FACES, NF, NF), F32),
            pltpu.VMEM((NI, FACES * MODES), F32),
            pltpu.VMEM((NI, FACES * MODES), F32),
        ],
        compiler_params=pltpu.CompilerParams(vmem_limit_bytes=32 << 20),
        cost_estimate=pl.CostEstimate(flops=4 << 30, bytes_accessed=4 << 20, transcendentals=0),
        name="coarse_partial",
    )(links, own, *received, modes, couple, solved, faces, owners)


def swap_pairs(value, axis, first):
    count = lax.axis_size(axis)
    pairs = []
    for low in range(first, count - 1, 2):
        pairs += [(low, low + 1), (low + 1, low)]
    return lax.ppermute(value, axis, pairs)


def shifted(value, axis, steps):
    count = lax.axis_size(axis)
    initial, last = (max(0, -steps), min(count, count - steps))
    return lax.ppermute(value, axis, [(source, source + steps) for source in range(initial, last)])


def body(interior_inverse, coupling, face_matrix, face_modes, face_links, owner_map):
    inverse = interior_inverse[0, 0]
    couple = coupling[0, 0]
    faces = face_matrix[0, 0]
    modes = face_modes[0, 0]
    links = face_links[0, 0]
    owners = owner_map[0]
    solved, own, north, south, far, near = own_blocks(inverse, couple, faces)
    far_part = swap_pairs(far, "gy", 1)
    north_part = shifted(south, "gx", 1)
    south_part = shifted(north, "gx", -1)
    near_part = swap_pairs(near, "gy", 0)
    received = (north_part, south_part, far_part, near_part)
    deluxe, partial = coarse_partial(links, own, received, modes, couple, solved, faces, owners)
    count = lax.axis_size("gy")
    parts = partial.reshape(count, NCG // count, FACES * MODES)
    coarse = lax.all_to_all(parts, "gy", 0, 0).sum(0)
    return deluxe[None, None], coarse[None]


def solution(mesh):
    placed = (
        P("gx", "gy", None, None),
        P("gx", "gy", None, None),
        P("gx", "gy", None, None, None),
        P("gx", "gy", None, None),
        P("gx", "gy", None),
        P("gx", "gy", None),
    )
    return jax.shard_map(
        body,
        mesh=mesh,
        in_specs=placed,
        out_specs=(P("gx", "gy", None, None, None), P("gx", "gy", None)),
        check_vma=False,
    )
```

```python
import jax
import jax.numpy as jnp
from jax import lax
from jax.experimental import pallas as pl
from jax.experimental.pallas import tpu as pltpu
from jax.sharding import PartitionSpec as P


NI = 768
NF = 256
FACES = 4
MODES = 32
NCG = 256
HALF = NF // 2

F32 = jnp.float32
BF16 = jnp.bfloat16
NORTH, SOUTH, WEST, EAST = range(FACES)

SWEEP_TOL = 3e-4
RESIDUAL_TOL = 4e-10
BOUND = 2e-5
MAX_SQUARINGS = 40
MAX_SWEEPS = 12


def dot(left, right):
    return lax.dot_general(left, right, (((1,), (0,)), ((), ())), preferred_element_type=F32)


def dot_rows(left, right):
    return lax.dot_general(left, right, (((0,), (0,)), ((), ())), preferred_element_type=F32)


def split(value):
    high = value.astype(BF16)
    return high, (value - high.astype(F32)).astype(BF16)


def left_three(value):
    high, low = split(value)
    return jnp.concatenate([high, high, low], axis=1)


def right_three(value):
    high, low = split(value)
    return jnp.concatenate([high, low, high], axis=0)


def odd_column():
    return lax.rem(lax.axis_index("gy"), 2) == 1


def grid_iota(rows, columns, dimension):
    return lax.broadcasted_iota(jnp.int32, (rows, columns), dimension)


def pack(block):
    first, last = block[:HALF, :HALF], block[HALF:, HALF:]
    rows, columns = grid_iota(HALF, HALF, 0), grid_iota(HALF, HALF, 1)
    diagonal = jnp.sum(jnp.where(rows == columns, last, 0.0), axis=0, keepdims=True)
    square = jnp.where(rows >= columns, first, last)
    return square, block[:HALF, HALF:], jnp.broadcast_to(diagonal, (8, HALF))


def unpack(packed):
    square, corner, diagonal = packed[:HALF], packed[HALF:NF], packed[NF : NF + 1]
    rows, columns = grid_iota(HALF, HALF, 0), grid_iota(HALF, HALF, 1)
    turned = square.T
    first = jnp.where(rows >= columns, square, turned)
    last = jnp.where(rows == columns, diagonal, jnp.where(rows < columns, square, turned))
    return first, corner, corner.T, last


def own_kernel(
    inverse_hbm, couple_hbm, faces_hbm,
    couple, solved, faces, own, send_north, send_south, send_far, send_near,
    inverse, sems,
):
    half = 2 * NF
    third = NI // 3

    def couple_copy(first, at):
        columns = slice(first, first + half)
        return pltpu.make_async_copy(couple_hbm.at[:, columns], couple.at[:, columns], sems.at[at])

    left, right = couple_copy(half, 0), couple_copy(0, 1)
    rows = [slice(n * third, (n + 1) * third) for n in range(3)]
    blocks = [
        pltpu.make_async_copy(inverse_hbm.at[here], inverse.at[here], sems.at[2 + n])
        for n, here in enumerate(rows)
    ]
    faces_copy = pltpu.make_async_copy(faces_hbm, faces, sems.at[5])
    for copy in [left, *blocks, faces_copy, right]:
        copy.start()
    left.wait()
    for block, here in zip(blocks, rows, strict=True):
        block.wait()
        solved[here, half:] = dot(inverse[here, :], couple[:, half:]).astype(BF16)
    faces_copy.wait()

    def own_of(n):
        columns = slice(n * NF, (n + 1) * NF)
        gram = dot_rows(couple[:, columns], solved[:, columns])
        block = faces[n].astype(F32) - 0.5 * (gram + gram.T)
        own[n] = block
        return pack(block)

    def put(ref, parts):
        ref[:HALF], ref[HALF:NF], ref[NF:] = parts

    odd = odd_column()
    pairs = list(zip(own_of(WEST), own_of(EAST), strict=True))
    put(send_far, [jnp.where(odd, e, w) for w, e in pairs])
    put(send_near, [jnp.where(odd, w, e) for w, e in pairs])
    right.wait()
    solved[:, :half] = dot(inverse[...], couple[:, :half]).astype(BF16)
    put(send_north, own_of(NORTH))
    put(send_south, own_of(SOUTH))


def own_blocks(inverse, couple, faces):
    vmem = pl.BlockSpec(memory_space=pltpu.VMEM)
    hbm = pl.BlockSpec(memory_space=pltpu.HBM)
    send = jax.ShapeDtypeStruct((NF + 8, HALF), F32)
    return pl.pallas_call(
        own_kernel,
        out_shape=(
            jax.ShapeDtypeStruct((NI, FACES * NF), BF16),
            jax.ShapeDtypeStruct((NI, FACES * NF), BF16),
            jax.ShapeDtypeStruct((FACES, NF, NF), BF16),
            jax.ShapeDtypeStruct((FACES, NF, NF), F32),
            send, send, send, send,
        ),
        in_specs=[hbm] * 3,
        out_specs=(vmem,) * 8,
        scratch_shapes=[pltpu.VMEM((NI, NI), BF16), pltpu.SemaphoreType.DMA((6,))],
        compiler_params=pltpu.CompilerParams(vmem_limit_bytes=20 << 20),
        name="own_blocks",
    )(*(pltpu.with_memory_space_constraint(value, pltpu.HBM) for value in (inverse, couple, faces)))


def eye():
    rows = lax.broadcasted_iota(jnp.int32, (NF, NF), 0)
    columns = lax.broadcasted_iota(jnp.int32, (NF, NF), 1)
    return rows == columns


def largest(values):
    result = values[0]
    for value in values[1:]:
        result = jnp.maximum(result, value)
    return result


def total_square(value):
    rows = jnp.sum(value * value, axis=0, keepdims=True)
    return jnp.sum(rows, axis=1, keepdims=True)


def general_solve(own, deluxe, matrix, scale, sweep, rest, power):
    own_norm = []
    for n in range(2):
        m, block = matrix[n], own[n]
        by = 1.0 / jnp.sum(jnp.where(eye(), m, 0.0), axis=1, keepdims=True)
        bound = jnp.max(jnp.sum(jnp.abs(m), axis=1, keepdims=True) * by)
        factor = jnp.where(bound < 1.75, 1.0, 1.0 / bound)
        scale[n] = jnp.broadcast_to(by * factor, (NF, HALF))
        rest[n] = block
        deluxe[n] = jnp.zeros((NF, NF), F32)
        own_norm.append(jnp.sum(block * block))

    def sweep_once(state):
        count, _, now = state
        for n in range(2):
            by = jnp.concatenate([scale[n]] * 2, axis=1)
            power[n] = jnp.where(eye(), 1.0, 0.0) - by * matrix[n]
            sweep[n] = by * rest[n]

        def more(inner):
            return jnp.logical_and(inner[1] > SWEEP_TOL, inner[0] < MAX_SQUARINGS)

        def squaring(inner):
            found = []
            for n in range(2):
                error = power[n]
                start = sweep[n]
                both = dot(left_three(error), right_three(jnp.concatenate([error, start], axis=1)))
                square = both[:, :NF]
                power[n] = square
                sweep[n] = start + both[:, NF:]
                found.append(jnp.sum(square * square))
            return inner[0] + 1, largest(found)

        lax.while_loop(more, squaring, (jnp.int32(0), jnp.float32(1.0)))

        ratios = []
        for n in range(2):
            start = sweep[n]
            total = deluxe[n] + (start + dot(left_three(power[n]), right_three(start)))
            deluxe[n] = total
            residual = own[n] - dot(left_three(matrix[n]), right_three(total))
            rest[n] = residual
            ratios.append(jnp.sum(residual * residual) / own_norm[n])
        return count + 1, now, largest(ratios)

    def unsolved(state):
        count, before, now = state
        return jnp.logical_and(
            jnp.logical_and(now > RESIDUAL_TOL, now < 0.25 * before), count < MAX_SWEEPS
        )

    lax.while_loop(unsolved, sweep_once, (jnp.int32(0), jnp.float32(8.0), jnp.float32(1.0)))


def face_weights(links):
    return [links[n].astype(F32) for n in range(FACES)]


def solve_pair(first, weight, own, packed, modes, couple, solved, faces, deluxe, scratch):
    matrix, scale, power, sweep, rest, general, phi = scratch
    own = own.at[first : first + 2]
    for n in range(2):
        quarters = unpack(packed[n])
        for at, quarter in enumerate(quarters):
            here = (slice((at // 2) * HALF, (at // 2 + 1) * HALF), slice((at % 2) * HALF, (at % 2 + 1) * HALF))
            matrix[(n, *here)] = own[(n, *here)] + quarter * weight[first + n]

    norms = [[] for _ in range(2)]
    for n in range(2):
        by = 1.0 / jnp.sum(jnp.where(eye(), matrix[n], 0.0), axis=1, keepdims=True)
        scale[n] = jnp.broadcast_to(by, (NF, HALF))
        factor = jnp.where(eye(), 0.0, -by * matrix[n])
        norms[n].append(total_square(factor))
        start = by * own[n]
        power[0, n] = factor.astype(BF16)
        both = dot(power[0, n], jnp.concatenate([power[0, n], start.astype(BF16)], axis=1))
        square = both[:, :NF]
        norms[n].append(total_square(square))
        power[1, n] = square.astype(BF16)
        sweep[n] = start + both[:, NF:]
    for n in range(2):
        start = sweep[n]
        rounded = (start + dot(power[1, n], start.astype(BF16))).astype(BF16)
        high, low = split(matrix[n])
        residual = own[n] - (dot(high, rounded) + dot(low, rounded))
        rest[n] = jnp.concatenate([scale[n]] * 2, axis=1) * residual
        rounded = rounded.astype(F32)
        norms[n].append(total_square(rounded))
        deluxe[n] = rounded
    for n in range(2):
        start = rest[n]
        sweep[n] = start + dot(power[0, n], start.astype(BF16))
    left_out = []
    for n in range(2):
        start = sweep[n]
        step = start + dot(power[1, n], start.astype(BF16))
        deluxe[n] = deluxe[n] + step
        one, two, size = (jnp.sqrt(norm) for norm in norms[n])
        rate = norms[n][1] + (one + two) * (1.0 + one) * 2.0**-8
        left_out.append(rate * jnp.sqrt(total_square(step)) / size)

    @pl.when(jnp.logical_not(jnp.max(largest(left_out)) < BOUND))
    def _():
        general_solve(own, deluxe, matrix, scale, sweep, rest, general)

    face_of = grid_iota(NF, FACES * MODES, 1) // MODES
    all_phi = jnp.zeros((NF, FACES * MODES), F32)
    for n in range(2):
        mode = jnp.where(face_of == first + n, modes[...].astype(F32), 0.0).astype(BF16)
        mapped = dot(
            jnp.concatenate(split(deluxe[n]), axis=1), jnp.concatenate([mode, mode], axis=0)
        )
        all_phi = all_phi + mapped
        phi[n * NF : (n + 1) * NF, :] = jnp.concatenate(split(mapped), axis=1)

    def times_phi(left):
        both = dot(left, phi[...])
        return both[:, : FACES * MODES] + both[:, FACES * MODES :]

    columns = slice(first * NF, (first + 2) * NF)
    return (
        times_phi(couple[:, columns]),
        times_phi(solved[:, columns]),
        times_phi(jnp.concatenate([faces[first], faces[first + 1]], axis=1)),
        all_phi,
    )


def columns_kernel(
    links, own, far, near, modes, couple, solved, faces,
    deluxe, left, right, faces_phi, all_phi,
    *scratch,
):
    odd = odd_column()
    packed = [jnp.where(odd, near[...], far[...]), jnp.where(odd, far[...], near[...])]
    left[...], right[...], faces_phi[...], all_phi[...] = solve_pair(
        WEST, face_weights(links), own, packed, modes, couple, solved, faces, deluxe, scratch
    )


def rows_kernel(
    links, own, north, south, modes, couple, solved, faces, owners,
    deluxe_we, left_we, right_we, faces_phi_we, all_phi_we,
    deluxe_hbm, partial,
    deluxe, *scratch_sems,
):
    *scratch, sems = scratch_sems
    weight = face_weights(links)
    out_we = pltpu.make_async_copy(deluxe_we, deluxe_hbm.at[WEST:], sems.at[1])
    out_we.start()
    packed = [north[...], south[...]]
    left, right, faces_phi, all_phi = solve_pair(
        NORTH, weight, own, packed, modes, couple, solved, faces, deluxe, scratch
    )
    out = pltpu.make_async_copy(deluxe, deluxe_hbm.at[:WEST], sems.at[0])
    out.start()
    cross = dot_three_rows(left + left_we[...], right + right_we[...])
    own_part = dot_three_rows(all_phi + all_phi_we[...], faces_phi + faces_phi_we[...])
    rows = grid_iota(FACES * MODES, FACES * MODES, 0)
    columns = grid_iota(FACES * MODES, FACES * MODES, 1)
    same = (rows // MODES) == (columns // MODES)
    local = jnp.where(same, own_part, 0.0) - 0.5 * (cross + cross.T)

    def spread(index):
        face = index // MODES
        value = jnp.zeros(index.shape, F32)
        for n in range(FACES):
            value = jnp.where(face == n, weight[n], value)
        return value

    local = local * spread(rows) * spread(columns)
    slots = lax.broadcasted_iota(jnp.int32, (NCG, FACES * MODES), 0)
    onehot = jnp.where(owners[...] == slots, 1.0, 0.0).astype(BF16)
    high, low = split(local)
    lowest = (local - high.astype(F32) - low.astype(F32)).astype(BF16)
    partial[...] = dot(onehot, high) + (dot(onehot, low) + dot(onehot, lowest))
    out_we.wait()
    out.wait()


def dot_three_rows(one, two):
    one_high, one_low = split(one)
    two_high, two_low = split(two)
    return dot_rows(one_high, two_high) + (dot_rows(one_high, two_low) + dot_rows(one_low, two_high))


VMEM_SPEC = pl.BlockSpec(memory_space=pltpu.VMEM)
SMEM_SPEC = pl.BlockSpec(memory_space=pltpu.SMEM)


def pair_scratch():
    square = pltpu.VMEM((2, NF, NF), F32)
    return [
        square,
        pltpu.VMEM((2, NF, HALF), F32),
        pltpu.VMEM((2, 2, NF, NF), BF16),
        square,
        square,
        square,
        pltpu.VMEM((2 * NF, 2 * FACES * MODES), BF16),
    ]


def columns_pair(links, own, far, near, modes, couple, solved, faces):
    tall = jax.ShapeDtypeStruct((NI, FACES * MODES), F32)
    short = jax.ShapeDtypeStruct((NF, FACES * MODES), F32)
    return pl.pallas_call(
        columns_kernel,
        out_shape=(jax.ShapeDtypeStruct((2, NF, NF), F32), tall, tall, short, short),
        in_specs=[SMEM_SPEC] + [VMEM_SPEC] * 7,
        out_specs=(VMEM_SPEC,) * 5,
        scratch_shapes=pair_scratch(),
        compiler_params=pltpu.CompilerParams(vmem_limit_bytes=24 << 20),
        cost_estimate=pl.CostEstimate(flops=2 << 30, bytes_accessed=4 << 20, transcendentals=0),
        name="columns_pair",
    )(links, own, far, near, modes, couple, solved, faces)


def rows_pair(links, own, north, south, modes, couple, solved, faces, owners, of_columns):
    return pl.pallas_call(
        rows_kernel,
        out_shape=(
            jax.ShapeDtypeStruct((FACES, NF, NF), F32),
            jax.ShapeDtypeStruct((NCG, FACES * MODES), F32),
        ),
        in_specs=[SMEM_SPEC] + [VMEM_SPEC] * 13,
        out_specs=(pl.BlockSpec(memory_space=pltpu.HBM), VMEM_SPEC),
        scratch_shapes=[
            pltpu.VMEM((2, NF, NF), F32), *pair_scratch(), pltpu.SemaphoreType.DMA((2,)),
        ],
        compiler_params=pltpu.CompilerParams(vmem_limit_bytes=24 << 20),
        cost_estimate=pl.CostEstimate(flops=3 << 30, bytes_accessed=4 << 20, transcendentals=0),
        name="rows_pair",
    )(links, own, north, south, modes, couple, solved, faces, owners, *of_columns)


def swap_pairs(value, axis, first):
    count = lax.axis_size(axis)
    pairs = []
    for low in range(first, count - 1, 2):
        pairs += [(low, low + 1), (low + 1, low)]
    return lax.ppermute(value, axis, pairs)


def shifted(value, axis, steps):
    count = lax.axis_size(axis)
    initial, last = (max(0, -steps), min(count, count - steps))
    return lax.ppermute(value, axis, [(source, source + steps) for source in range(initial, last)])


def body(interior_inverse, coupling, face_matrix, face_modes, face_links, owner_map):
    inverse = interior_inverse[0, 0]
    couple = coupling[0, 0]
    faces = face_matrix[0, 0]
    modes = face_modes[0, 0]
    links = face_links[0, 0]
    owners = owner_map[0]
    couple, solved, faces, own, north, south, far, near = own_blocks(inverse, couple, faces)
    far_part = swap_pairs(far, "gy", 1)
    near_part = swap_pairs(near, "gy", 0)
    north_part = shifted(south, "gx", 1)
    south_part = shifted(north, "gx", -1)
    of_columns = columns_pair(links, own, far_part, near_part, modes, couple, solved, faces)
    deluxe, partial = rows_pair(
        links, own, north_part, south_part, modes, couple, solved, faces, owners, of_columns
    )
    count = lax.axis_size("gy")
    parts = partial.reshape(count, NCG // count, FACES * MODES)
    coarse = lax.all_to_all(parts, "gy", 0, 0).sum(0)
    return deluxe[None, None], coarse[None]


def solution(mesh):
    placed = (
        P("gx", "gy", None, None),
        P("gx", "gy", None, None),
        P("gx", "gy", None, None, None),
        P("gx", "gy", None, None),
        P("gx", "gy", None),
        P("gx", "gy", None),
    )
    return jax.shard_map(
        body,
        mesh=mesh,
        in_specs=placed,
        out_specs=(P("gx", "gy", None, None, None), P("gx", "gy", None)),
        check_vma=False,
    )
```

```python
import jax
import jax.numpy as jnp
from jax import lax
from jax.experimental import pallas as pl
from jax.experimental.pallas import tpu as pltpu
from jax.sharding import PartitionSpec as P


NI = 768
NF = 256
FACES = 4
MODES = 32
NCG = 256
HALF = NF // 2

F32 = jnp.float32
BF16 = jnp.bfloat16
NORTH, SOUTH, WEST, EAST = range(FACES)

SWEEP_TOL = 3e-4
RESIDUAL_TOL = 4e-10
BOUND = 2e-5
MAX_SQUARINGS = 40
MAX_SWEEPS = 12


def dot(left, right):
    return lax.dot_general(left, right, (((1,), (0,)), ((), ())), preferred_element_type=F32)


def dot_rows(left, right):
    return lax.dot_general(left, right, (((0,), (0,)), ((), ())), preferred_element_type=F32)


def split(value):
    high = value.astype(BF16)
    return high, (value - high.astype(F32)).astype(BF16)


def left_three(value):
    high, low = split(value)
    return jnp.concatenate([high, high, low], axis=1)


def right_three(value):
    high, low = split(value)
    return jnp.concatenate([high, low, high], axis=0)


def odd_at(axis):
    return lax.rem(lax.axis_index(axis), 2) == 1


def grid_iota(rows, columns, dimension):
    return lax.broadcasted_iota(jnp.int32, (rows, columns), dimension)


def pack(block):
    first, last = block[:HALF, :HALF], block[HALF:, HALF:]
    rows, columns = grid_iota(HALF, HALF, 0), grid_iota(HALF, HALF, 1)
    diagonal = jnp.sum(jnp.where(rows == columns, last, 0.0), axis=0, keepdims=True)
    square = jnp.where(rows >= columns, first, last)
    return square, block[:HALF, HALF:], jnp.broadcast_to(diagonal, (8, HALF))


def unpack(packed):
    square, corner, diagonal = packed[:HALF], packed[HALF:NF], packed[NF : NF + 1]
    rows, columns = grid_iota(HALF, HALF, 0), grid_iota(HALF, HALF, 1)
    turned = square.T
    first = jnp.where(rows >= columns, square, turned)
    last = jnp.where(rows == columns, diagonal, jnp.where(rows < columns, square, turned))
    return first, corner, corner.T, last


def own_kernel(
    inverse_hbm, couple_hbm, faces_hbm,
    couple, solved, faces, own, send_even, send_odd, send_far, send_near,
    inverse, sems,
):
    half = 2 * NF
    third = NI // 3

    def couple_copy(first, at):
        columns = slice(first, first + half)
        return pltpu.make_async_copy(couple_hbm.at[:, columns], couple.at[:, columns], sems.at[at])

    left, right = couple_copy(half, 0), couple_copy(0, 1)
    rows = [slice(n * third, (n + 1) * third) for n in range(3)]
    blocks = [
        pltpu.make_async_copy(inverse_hbm.at[here], inverse.at[here], sems.at[2 + n])
        for n, here in enumerate(rows)
    ]
    faces_copy = pltpu.make_async_copy(faces_hbm, faces, sems.at[5])
    for copy in [left, *blocks, faces_copy, right]:
        copy.start()
    left.wait()
    for block, here in zip(blocks, rows, strict=True):
        block.wait()
        solved[here, half:] = dot(inverse[here, :], couple[:, half:]).astype(BF16)
    faces_copy.wait()

    def own_of(n):
        columns = slice(n * NF, (n + 1) * NF)
        gram = dot_rows(couple[:, columns], solved[:, columns])
        block = faces[n].astype(F32) - 0.5 * (gram + gram.T)
        own[n] = block
        return pack(block)

    def put(ref, parts):
        ref[:HALF], ref[HALF:NF], ref[NF:] = parts

    def put_pair(odd, low, high, up, down):
        pairs = list(zip(low, high, strict=True))
        put(up, [jnp.where(odd, l, h) for l, h in pairs])
        put(down, [jnp.where(odd, h, l) for l, h in pairs])

    put_pair(odd_at("gy"), own_of(WEST), own_of(EAST), send_near, send_far)
    right.wait()
    solved[:, :half] = dot(inverse[...], couple[:, :half]).astype(BF16)
    put_pair(odd_at("gx"), own_of(NORTH), own_of(SOUTH), send_even, send_odd)


def own_blocks(inverse, couple, faces):
    vmem = pl.BlockSpec(memory_space=pltpu.VMEM)
    hbm = pl.BlockSpec(memory_space=pltpu.HBM)
    send = jax.ShapeDtypeStruct((NF + 8, HALF), F32)
    return pl.pallas_call(
        own_kernel,
        out_shape=(
            jax.ShapeDtypeStruct((NI, FACES * NF), BF16),
            jax.ShapeDtypeStruct((NI, FACES * NF), BF16),
            jax.ShapeDtypeStruct((FACES, NF, NF), BF16),
            jax.ShapeDtypeStruct((FACES, NF, NF), F32),
            send, send, send, send,
        ),
        in_specs=[hbm] * 3,
        out_specs=(vmem,) * 8,
        scratch_shapes=[pltpu.VMEM((NI, NI), BF16), pltpu.SemaphoreType.DMA((6,))],
        compiler_params=pltpu.CompilerParams(vmem_limit_bytes=20 << 20),
        name="own_blocks",
    )(*(pltpu.with_memory_space_constraint(value, pltpu.HBM) for value in (inverse, couple, faces)))


def eye():
    rows = lax.broadcasted_iota(jnp.int32, (NF, NF), 0)
    columns = lax.broadcasted_iota(jnp.int32, (NF, NF), 1)
    return rows == columns


def largest(values):
    result = values[0]
    for value in values[1:]:
        result = jnp.maximum(result, value)
    return result


def total_square(value):
    rows = jnp.sum(value * value, axis=0, keepdims=True)
    return jnp.sum(rows, axis=1, keepdims=True)


def general_solve(own, deluxe, matrix, scale, sweep, rest, power):
    own_norm = []
    for n in range(2):
        m, block = matrix[n], own[n]
        by = 1.0 / jnp.sum(jnp.where(eye(), m, 0.0), axis=1, keepdims=True)
        bound = jnp.max(jnp.sum(jnp.abs(m), axis=1, keepdims=True) * by)
        factor = jnp.where(bound < 1.75, 1.0, 1.0 / bound)
        scale[n] = jnp.broadcast_to(by * factor, (NF, HALF))
        rest[n] = block
        deluxe[n] = jnp.zeros((NF, NF), F32)
        own_norm.append(jnp.sum(block * block))

    def sweep_once(state):
        count, _, now = state
        for n in range(2):
            by = jnp.concatenate([scale[n]] * 2, axis=1)
            power[n] = jnp.where(eye(), 1.0, 0.0) - by * matrix[n]
            sweep[n] = by * rest[n]

        def more(inner):
            return jnp.logical_and(inner[1] > SWEEP_TOL, inner[0] < MAX_SQUARINGS)

        def squaring(inner):
            found = []
            for n in range(2):
                error = power[n]
                start = sweep[n]
                both = dot(left_three(error), right_three(jnp.concatenate([error, start], axis=1)))
                square = both[:, :NF]
                power[n] = square
                sweep[n] = start + both[:, NF:]
                found.append(jnp.sum(square * square))
            return inner[0] + 1, largest(found)

        lax.while_loop(more, squaring, (jnp.int32(0), jnp.float32(1.0)))

        ratios = []
        for n in range(2):
            start = sweep[n]
            total = deluxe[n] + (start + dot(left_three(power[n]), right_three(start)))
            deluxe[n] = total
            residual = own[n] - dot(left_three(matrix[n]), right_three(total))
            rest[n] = residual
            ratios.append(jnp.sum(residual * residual) / own_norm[n])
        return count + 1, now, largest(ratios)

    def unsolved(state):
        count, before, now = state
        return jnp.logical_and(
            jnp.logical_and(now > RESIDUAL_TOL, now < 0.25 * before), count < MAX_SWEEPS
        )

    lax.while_loop(unsolved, sweep_once, (jnp.int32(0), jnp.float32(8.0), jnp.float32(1.0)))


def face_weights(links):
    return [links[n].astype(F32) for n in range(FACES)]


def solve_pair(first, weight, own, packed, modes, couple, solved, faces, deluxe, scratch):
    matrix, scale, power, sweep, rest, general, phi = scratch
    own = own.at[first : first + 2]
    for n in range(2):
        quarters = unpack(packed[n])
        for at, quarter in enumerate(quarters):
            here = (slice((at // 2) * HALF, (at // 2 + 1) * HALF), slice((at % 2) * HALF, (at % 2 + 1) * HALF))
            matrix[(n, *here)] = own[(n, *here)] + quarter * weight[first + n]

    norms = [[] for _ in range(2)]
    for n in range(2):
        by = 1.0 / jnp.sum(jnp.where(eye(), matrix[n], 0.0), axis=1, keepdims=True)
        scale[n] = jnp.broadcast_to(by, (NF, HALF))
        factor = jnp.where(eye(), 0.0, -by * matrix[n])
        norms[n].append(total_square(factor))
        start = by * own[n]
        power[0, n] = factor.astype(BF16)
        both = dot(power[0, n], jnp.concatenate([power[0, n], start.astype(BF16)], axis=1))
        square = both[:, :NF]
        norms[n].append(total_square(square))
        power[1, n] = square.astype(BF16)
        sweep[n] = start + both[:, NF:]
    for n in range(2):
        start = sweep[n]
        rounded = (start + dot(power[1, n], start.astype(BF16))).astype(BF16)
        high, low = split(matrix[n])
        residual = own[n] - (dot(high, rounded) + dot(low, rounded))
        rest[n] = jnp.concatenate([scale[n]] * 2, axis=1) * residual
        rounded = rounded.astype(F32)
        norms[n].append(total_square(rounded))
        deluxe[n] = rounded
    for n in range(2):
        start = rest[n]
        sweep[n] = start + dot(power[0, n], start.astype(BF16))
    left_out = []
    for n in range(2):
        start = sweep[n]
        step = start + dot(power[1, n], start.astype(BF16))
        deluxe[n] = deluxe[n] + step
        one, two, size = (jnp.sqrt(norm) for norm in norms[n])
        rate = norms[n][1] + (one + two) * (1.0 + one) * 2.0**-8
        left_out.append(rate * jnp.sqrt(total_square(step)) / size)

    @pl.when(jnp.logical_not(jnp.max(largest(left_out)) < BOUND))
    def _():
        general_solve(own, deluxe, matrix, scale, sweep, rest, general)

    face_of = grid_iota(NF, FACES * MODES, 1) // MODES
    all_phi = jnp.zeros((NF, FACES * MODES), F32)
    for n in range(2):
        mode = jnp.where(face_of == first + n, modes[...].astype(F32), 0.0).astype(BF16)
        mapped = dot(
            jnp.concatenate(split(deluxe[n]), axis=1), jnp.concatenate([mode, mode], axis=0)
        )
        all_phi = all_phi + mapped
        phi[n * NF : (n + 1) * NF, :] = jnp.concatenate(split(mapped), axis=1)

    def times_phi(left):
        both = dot(left, phi[...])
        return both[:, : FACES * MODES] + both[:, FACES * MODES :]

    columns = slice(first * NF, (first + 2) * NF)
    return (
        times_phi(couple[:, columns]),
        times_phi(solved[:, columns]),
        times_phi(jnp.concatenate([faces[first], faces[first + 1]], axis=1)),
        all_phi,
    )


def columns_kernel(
    links, own, far, near, modes, couple, solved, faces,
    deluxe, left, right, faces_phi, all_phi,
    *scratch,
):
    odd = odd_at("gy")
    packed = [jnp.where(odd, near[...], far[...]), jnp.where(odd, far[...], near[...])]
    left[...], right[...], faces_phi[...], all_phi[...] = solve_pair(
        WEST, face_weights(links), own, packed, modes, couple, solved, faces, deluxe, scratch
    )


def rows_kernel(
    links, own, even, other, modes, couple, solved, faces, owners,
    deluxe_we, left_we, right_we, faces_phi_we, all_phi_we,
    deluxe_hbm, partial,
    deluxe, *scratch_sems,
):
    *scratch, sems = scratch_sems
    weight = face_weights(links)
    out_we = pltpu.make_async_copy(deluxe_we, deluxe_hbm.at[WEST:], sems.at[1])
    out_we.start()
    odd = odd_at("gx")
    packed = [jnp.where(odd, even[...], other[...]), jnp.where(odd, other[...], even[...])]
    left, right, faces_phi, all_phi = solve_pair(
        NORTH, weight, own, packed, modes, couple, solved, faces, deluxe, scratch
    )
    out = pltpu.make_async_copy(deluxe, deluxe_hbm.at[:WEST], sems.at[0])
    out.start()
    cross = dot_three_rows(left + left_we[...], right + right_we[...])
    own_part = dot_three_rows(all_phi + all_phi_we[...], faces_phi + faces_phi_we[...])
    rows = grid_iota(FACES * MODES, FACES * MODES, 0)
    columns = grid_iota(FACES * MODES, FACES * MODES, 1)
    same = (rows // MODES) == (columns // MODES)
    local = jnp.where(same, own_part, 0.0) - 0.5 * (cross + cross.T)

    def spread(index):
        face = index // MODES
        value = jnp.zeros(index.shape, F32)
        for n in range(FACES):
            value = jnp.where(face == n, weight[n], value)
        return value

    local = local * spread(rows) * spread(columns)
    slots = lax.broadcasted_iota(jnp.int32, (NCG, FACES * MODES), 0)
    onehot = jnp.where(owners[...] == slots, 1.0, 0.0).astype(BF16)
    high, low = split(local)
    lowest = (local - high.astype(F32) - low.astype(F32)).astype(BF16)
    partial[...] = dot(onehot, high) + (dot(onehot, low) + dot(onehot, lowest))
    out_we.wait()
    out.wait()


def dot_three_rows(one, two):
    one_high, one_low = split(one)
    two_high, two_low = split(two)
    return dot_rows(one_high, two_high) + (dot_rows(one_high, two_low) + dot_rows(one_low, two_high))


VMEM_SPEC = pl.BlockSpec(memory_space=pltpu.VMEM)
SMEM_SPEC = pl.BlockSpec(memory_space=pltpu.SMEM)


def pair_scratch():
    square = pltpu.VMEM((2, NF, NF), F32)
    return [
        square,
        pltpu.VMEM((2, NF, HALF), F32),
        pltpu.VMEM((2, 2, NF, NF), BF16),
        square,
        square,
        square,
        pltpu.VMEM((2 * NF, 2 * FACES * MODES), BF16),
    ]


def columns_pair(links, own, far, near, modes, couple, solved, faces):
    tall = jax.ShapeDtypeStruct((NI, FACES * MODES), F32)
    short = jax.ShapeDtypeStruct((NF, FACES * MODES), F32)
    return pl.pallas_call(
        columns_kernel,
        out_shape=(jax.ShapeDtypeStruct((2, NF, NF), F32), tall, tall, short, short),
        in_specs=[SMEM_SPEC] + [VMEM_SPEC] * 7,
        out_specs=(VMEM_SPEC,) * 5,
        scratch_shapes=pair_scratch(),
        compiler_params=pltpu.CompilerParams(vmem_limit_bytes=24 << 20),
        cost_estimate=pl.CostEstimate(flops=2 << 30, bytes_accessed=4 << 20, transcendentals=0),
        name="columns_pair",
    )(links, own, far, near, modes, couple, solved, faces)


def rows_pair(links, own, even, other, modes, couple, solved, faces, owners, of_columns):
    return pl.pallas_call(
        rows_kernel,
        out_shape=(
            jax.ShapeDtypeStruct((FACES, NF, NF), F32),
            jax.ShapeDtypeStruct((NCG, FACES * MODES), F32),
        ),
        in_specs=[SMEM_SPEC] + [VMEM_SPEC] * 13,
        out_specs=(pl.BlockSpec(memory_space=pltpu.HBM), VMEM_SPEC),
        scratch_shapes=[
            pltpu.VMEM((2, NF, NF), F32), *pair_scratch(), pltpu.SemaphoreType.DMA((2,)),
        ],
        compiler_params=pltpu.CompilerParams(vmem_limit_bytes=24 << 20),
        cost_estimate=pl.CostEstimate(flops=3 << 30, bytes_accessed=4 << 20, transcendentals=0),
        name="rows_pair",
    )(links, own, even, other, modes, couple, solved, faces, owners, *of_columns)


def swap_pairs(value, axis, first):
    count = lax.axis_size(axis)
    pairs = []
    for low in range(first, count - 1, 2):
        pairs += [(low, low + 1), (low + 1, low)]
    return lax.ppermute(value, axis, pairs)


def body(interior_inverse, coupling, face_matrix, face_modes, face_links, owner_map):
    inverse = interior_inverse[0, 0]
    couple = coupling[0, 0]
    faces = face_matrix[0, 0]
    modes = face_modes[0, 0]
    links = face_links[0, 0]
    owners = owner_map[0]
    couple, solved, faces, own, even, other, far, near = own_blocks(inverse, couple, faces)
    far_part = swap_pairs(far, "gy", 1)
    near_part = swap_pairs(near, "gy", 0)
    even_part = swap_pairs(even, "gx", 0)
    other_part = swap_pairs(other, "gx", 1)
    of_columns = columns_pair(links, own, far_part, near_part, modes, couple, solved, faces)
    deluxe, partial = rows_pair(
        links, own, even_part, other_part, modes, couple, solved, faces, owners, of_columns
    )
    count = lax.axis_size("gy")
    parts = partial.reshape(count, NCG // count, FACES * MODES)
    coarse = lax.all_to_all(parts, "gy", 0, 0).sum(0)
    return deluxe[None, None], coarse[None]


def solution(mesh):
    placed = (
        P("gx", "gy", None, None),
        P("gx", "gy", None, None),
        P("gx", "gy", None, None, None),
        P("gx", "gy", None, None),
        P("gx", "gy", None),
        P("gx", "gy", None),
    )
    return jax.shard_map(
        body,
        mesh=mesh,
        in_specs=placed,
        out_specs=(P("gx", "gy", None, None, None), P("gx", "gy", None)),
        check_vma=False,
    )
```

```python
import jax
import jax.numpy as jnp
from jax import lax
from jax.experimental import pallas as pl
from jax.experimental.pallas import tpu as pltpu
from jax.sharding import PartitionSpec as P


NI = 768
NF = 256
FACES = 4
MODES = 32
NCG = 256
HALF = NF // 2

F32 = jnp.float32
BF16 = jnp.bfloat16
NORTH, SOUTH, WEST, EAST = range(FACES)

SWEEP_TOL = 3e-4
RESIDUAL_TOL = 4e-10
BOUND = 2e-5
MAX_SQUARINGS = 40
MAX_SWEEPS = 12


def dot(left, right):
    return lax.dot_general(left, right, (((1,), (0,)), ((), ())), preferred_element_type=F32)


def dot_rows(left, right):
    return lax.dot_general(left, right, (((0,), (0,)), ((), ())), preferred_element_type=F32)


def split(value):
    high = value.astype(BF16)
    return high, (value - high.astype(F32)).astype(BF16)


def left_three(value):
    high, low = split(value)
    return jnp.concatenate([high, high, low], axis=1)


def right_three(value):
    high, low = split(value)
    return jnp.concatenate([high, low, high], axis=0)


def odd_at(axis):
    return lax.rem(lax.axis_index(axis), 2) == 1


def west_first():
    low = lax.axis_index("gx") < lax.axis_size("gx") // 2
    return odd_at("gy") == low


def grid_iota(rows, columns, dimension):
    return lax.broadcasted_iota(jnp.int32, (rows, columns), dimension)


def pack(block):
    first, last = block[:HALF, :HALF], block[HALF:, HALF:]
    rows, columns = grid_iota(HALF, HALF, 0), grid_iota(HALF, HALF, 1)
    diagonal = jnp.sum(jnp.where(rows == columns, last, 0.0), axis=0, keepdims=True)
    square = jnp.where(rows >= columns, first, last)
    return square, block[:HALF, HALF:], jnp.broadcast_to(diagonal, (8, HALF))


def unpack(packed):
    square, corner, diagonal = packed[:HALF], packed[HALF:NF], packed[NF : NF + 1]
    rows, columns = grid_iota(HALF, HALF, 0), grid_iota(HALF, HALF, 1)
    turned = square.T
    first = jnp.where(rows >= columns, square, turned)
    last = jnp.where(rows == columns, diagonal, jnp.where(rows < columns, square, turned))
    return first, corner, corner.T, last


def own_kernel(
    inverse_hbm, couple_hbm, faces_hbm,
    couple, solved, faces, own, send_even, send_odd, send_first, send_last,
    inverse, sems,
):
    half = 2 * NF
    third = NI // 3

    def couple_copy(first, at):
        columns = slice(first, first + half)
        return pltpu.make_async_copy(couple_hbm.at[:, columns], couple.at[:, columns], sems.at[at])

    left, right = couple_copy(half, 0), couple_copy(0, 1)
    rows = [slice(n * third, (n + 1) * third) for n in range(3)]
    blocks = [
        pltpu.make_async_copy(inverse_hbm.at[here], inverse.at[here], sems.at[2 + n])
        for n, here in enumerate(rows)
    ]
    faces_copy = pltpu.make_async_copy(faces_hbm, faces, sems.at[5])
    for copy in [left, *blocks, faces_copy, right]:
        copy.start()
    left.wait()
    for block, here in zip(blocks, rows, strict=True):
        block.wait()
        solved[here, half:] = dot(inverse[here, :], couple[:, half:]).astype(BF16)
    faces_copy.wait()

    def own_of(n):
        columns = slice(n * NF, (n + 1) * NF)
        gram = dot_rows(couple[:, columns], solved[:, columns])
        block = faces[n].astype(F32) - 0.5 * (gram + gram.T)
        own[n] = block
        return pack(block)

    def put(ref, parts):
        ref[:HALF], ref[HALF:NF], ref[NF:] = parts

    def put_pair(odd, low, high, up, down):
        pairs = list(zip(low, high, strict=True))
        put(up, [jnp.where(odd, l, h) for l, h in pairs])
        put(down, [jnp.where(odd, h, l) for l, h in pairs])

    put_pair(west_first(), own_of(WEST), own_of(EAST), send_first, send_last)
    right.wait()
    solved[:, :half] = dot(inverse[...], couple[:, :half]).astype(BF16)
    put_pair(odd_at("gx"), own_of(NORTH), own_of(SOUTH), send_even, send_odd)


def own_blocks(inverse, couple, faces):
    vmem = pl.BlockSpec(memory_space=pltpu.VMEM)
    hbm = pl.BlockSpec(memory_space=pltpu.HBM)
    send = jax.ShapeDtypeStruct((NF + 8, HALF), F32)
    return pl.pallas_call(
        own_kernel,
        out_shape=(
            jax.ShapeDtypeStruct((NI, FACES * NF), BF16),
            jax.ShapeDtypeStruct((NI, FACES * NF), BF16),
            jax.ShapeDtypeStruct((FACES, NF, NF), BF16),
            jax.ShapeDtypeStruct((FACES, NF, NF), F32),
            send, send, send, send,
        ),
        in_specs=[hbm] * 3,
        out_specs=(vmem,) * 8,
        scratch_shapes=[pltpu.VMEM((NI, NI), BF16), pltpu.SemaphoreType.DMA((6,))],
        compiler_params=pltpu.CompilerParams(vmem_limit_bytes=20 << 20),
        name="own_blocks",
    )(*(pltpu.with_memory_space_constraint(value, pltpu.HBM) for value in (inverse, couple, faces)))


def eye():
    rows = lax.broadcasted_iota(jnp.int32, (NF, NF), 0)
    columns = lax.broadcasted_iota(jnp.int32, (NF, NF), 1)
    return rows == columns


def largest(values):
    result = values[0]
    for value in values[1:]:
        result = jnp.maximum(result, value)
    return result


def total_square(value):
    rows = jnp.sum(value * value, axis=0, keepdims=True)
    return jnp.sum(rows, axis=1, keepdims=True)


def general_solve(own, deluxe, matrix, scale, sweep, rest, power):
    own_norm = []
    for n in range(2):
        m, block = matrix[n], own[n]
        by = 1.0 / jnp.sum(jnp.where(eye(), m, 0.0), axis=1, keepdims=True)
        bound = jnp.max(jnp.sum(jnp.abs(m), axis=1, keepdims=True) * by)
        factor = jnp.where(bound < 1.75, 1.0, 1.0 / bound)
        scale[n] = jnp.broadcast_to(by * factor, (NF, HALF))
        rest[n] = block
        deluxe[n] = jnp.zeros((NF, NF), F32)
        own_norm.append(jnp.sum(block * block))

    def sweep_once(state):
        count, _, now = state
        for n in range(2):
            by = jnp.concatenate([scale[n]] * 2, axis=1)
            power[n] = jnp.where(eye(), 1.0, 0.0) - by * matrix[n]
            sweep[n] = by * rest[n]

        def more(inner):
            return jnp.logical_and(inner[1] > SWEEP_TOL, inner[0] < MAX_SQUARINGS)

        def squaring(inner):
            found = []
            for n in range(2):
                error = power[n]
                start = sweep[n]
                both = dot(left_three(error), right_three(jnp.concatenate([error, start], axis=1)))
                square = both[:, :NF]
                power[n] = square
                sweep[n] = start + both[:, NF:]
                found.append(jnp.sum(square * square))
            return inner[0] + 1, largest(found)

        lax.while_loop(more, squaring, (jnp.int32(0), jnp.float32(1.0)))

        ratios = []
        for n in range(2):
            start = sweep[n]
            total = deluxe[n] + (start + dot(left_three(power[n]), right_three(start)))
            deluxe[n] = total
            residual = own[n] - dot(left_three(matrix[n]), right_three(total))
            rest[n] = residual
            ratios.append(jnp.sum(residual * residual) / own_norm[n])
        return count + 1, now, largest(ratios)

    def unsolved(state):
        count, before, now = state
        return jnp.logical_and(
            jnp.logical_and(now > RESIDUAL_TOL, now < 0.25 * before), count < MAX_SWEEPS
        )

    lax.while_loop(unsolved, sweep_once, (jnp.int32(0), jnp.float32(8.0), jnp.float32(1.0)))


def face_weights(links):
    return [links[n].astype(F32) for n in range(FACES)]


def solve_pair(first, weight, own, packed, modes, couple, solved, faces, deluxe, scratch):
    matrix, scale, power, sweep, rest, general, phi = scratch
    own = own.at[first : first + 2]
    for n in range(2):
        quarters = unpack(packed[n])
        for at, quarter in enumerate(quarters):
            here = (slice((at // 2) * HALF, (at // 2 + 1) * HALF), slice((at % 2) * HALF, (at % 2 + 1) * HALF))
            matrix[(n, *here)] = own[(n, *here)] + quarter * weight[first + n]

    norms = [[] for _ in range(2)]
    for n in range(2):
        by = 1.0 / jnp.sum(jnp.where(eye(), matrix[n], 0.0), axis=1, keepdims=True)
        scale[n] = jnp.broadcast_to(by, (NF, HALF))
        factor = jnp.where(eye(), 0.0, -by * matrix[n])
        norms[n].append(total_square(factor))
        start = by * own[n]
        power[0, n] = factor.astype(BF16)
        both = dot(power[0, n], jnp.concatenate([power[0, n], start.astype(BF16)], axis=1))
        square = both[:, :NF]
        norms[n].append(total_square(square))
        power[1, n] = square.astype(BF16)
        sweep[n] = start + both[:, NF:]
    for n in range(2):
        start = sweep[n]
        rounded = (start + dot(power[1, n], start.astype(BF16))).astype(BF16)
        high, low = split(matrix[n])
        residual = own[n] - (dot(high, rounded) + dot(low, rounded))
        rest[n] = jnp.concatenate([scale[n]] * 2, axis=1) * residual
        rounded = rounded.astype(F32)
        norms[n].append(total_square(rounded))
        deluxe[n] = rounded
    for n in range(2):
        start = rest[n]
        sweep[n] = start + dot(power[0, n], start.astype(BF16))
    left_out = []
    for n in range(2):
        start = sweep[n]
        step = start + dot(power[1, n], start.astype(BF16))
        deluxe[n] = deluxe[n] + step
        one, two, size = (jnp.sqrt(norm) for norm in norms[n])
        rate = norms[n][1] + (one + two) * (1.0 + one) * 2.0**-8
        left_out.append(rate * jnp.sqrt(total_square(step)) / size)

    @pl.when(jnp.logical_not(jnp.max(largest(left_out)) < BOUND))
    def _():
        general_solve(own, deluxe, matrix, scale, sweep, rest, general)

    face_of = grid_iota(NF, FACES * MODES, 1) // MODES
    all_phi = jnp.zeros((NF, FACES * MODES), F32)
    for n in range(2):
        mode = jnp.where(face_of == first + n, modes[...].astype(F32), 0.0).astype(BF16)
        mapped = dot(
            jnp.concatenate(split(deluxe[n]), axis=1), jnp.concatenate([mode, mode], axis=0)
        )
        all_phi = all_phi + mapped
        phi[n * NF : (n + 1) * NF, :] = jnp.concatenate(split(mapped), axis=1)

    def times_phi(left):
        both = dot(left, phi[...])
        return both[:, : FACES * MODES] + both[:, FACES * MODES :]

    columns = slice(first * NF, (first + 2) * NF)
    return (
        times_phi(couple[:, columns]),
        times_phi(solved[:, columns]),
        times_phi(jnp.concatenate([faces[first], faces[first + 1]], axis=1)),
        all_phi,
    )


def rows_kernel(
    links, own, even, other, modes, couple, solved, faces,
    deluxe, left, right, faces_phi, all_phi,
    *scratch,
):
    odd = odd_at("gx")
    packed = [jnp.where(odd, even[...], other[...]), jnp.where(odd, other[...], even[...])]
    left[...], right[...], faces_phi[...], all_phi[...] = solve_pair(
        NORTH, face_weights(links), own, packed, modes, couple, solved, faces, deluxe, scratch
    )


def columns_kernel(
    links, own, first, last, modes, couple, solved, faces, owners,
    deluxe_ns, left_ns, right_ns, faces_phi_ns, all_phi_ns,
    deluxe_hbm, partial,
    deluxe, *scratch_sems,
):
    *scratch, sems = scratch_sems
    weight = face_weights(links)
    out_ns = pltpu.make_async_copy(deluxe_ns, deluxe_hbm.at[:WEST], sems.at[1])
    out_ns.start()
    from_first = west_first()
    packed = [jnp.where(from_first, first[...], last[...]), jnp.where(from_first, last[...], first[...])]
    left, right, faces_phi, all_phi = solve_pair(
        WEST, weight, own, packed, modes, couple, solved, faces, deluxe, scratch
    )
    out = pltpu.make_async_copy(deluxe, deluxe_hbm.at[WEST:], sems.at[0])
    out.start()
    cross = dot_three_rows(left + left_ns[...], right + right_ns[...])
    own_part = dot_three_rows(all_phi + all_phi_ns[...], faces_phi + faces_phi_ns[...])
    rows = grid_iota(FACES * MODES, FACES * MODES, 0)
    columns = grid_iota(FACES * MODES, FACES * MODES, 1)
    same = (rows // MODES) == (columns // MODES)
    local = jnp.where(same, own_part, 0.0) - 0.5 * (cross + cross.T)

    def spread(index):
        face = index // MODES
        value = jnp.zeros(index.shape, F32)
        for n in range(FACES):
            value = jnp.where(face == n, weight[n], value)
        return value

    local = local * spread(rows) * spread(columns)
    slots = lax.broadcasted_iota(jnp.int32, (NCG, FACES * MODES), 0)
    onehot = jnp.where(owners[...] == slots, 1.0, 0.0).astype(BF16)
    high, low = split(local)
    lowest = (local - high.astype(F32) - low.astype(F32)).astype(BF16)
    partial[...] = dot(onehot, high) + (dot(onehot, low) + dot(onehot, lowest))
    out_ns.wait()
    out.wait()


def dot_three_rows(one, two):
    one_high, one_low = split(one)
    two_high, two_low = split(two)
    return dot_rows(one_high, two_high) + (dot_rows(one_high, two_low) + dot_rows(one_low, two_high))


VMEM_SPEC = pl.BlockSpec(memory_space=pltpu.VMEM)
SMEM_SPEC = pl.BlockSpec(memory_space=pltpu.SMEM)


def pair_scratch():
    square = pltpu.VMEM((2, NF, NF), F32)
    return [
        square,
        pltpu.VMEM((2, NF, HALF), F32),
        pltpu.VMEM((2, 2, NF, NF), BF16),
        square,
        square,
        square,
        pltpu.VMEM((2 * NF, 2 * FACES * MODES), BF16),
    ]


def rows_pair(links, own, even, other, modes, couple, solved, faces):
    tall = jax.ShapeDtypeStruct((NI, FACES * MODES), F32)
    short = jax.ShapeDtypeStruct((NF, FACES * MODES), F32)
    return pl.pallas_call(
        rows_kernel,
        out_shape=(jax.ShapeDtypeStruct((2, NF, NF), F32), tall, tall, short, short),
        in_specs=[SMEM_SPEC] + [VMEM_SPEC] * 7,
        out_specs=(VMEM_SPEC,) * 5,
        scratch_shapes=pair_scratch(),
        compiler_params=pltpu.CompilerParams(vmem_limit_bytes=24 << 20),
        cost_estimate=pl.CostEstimate(flops=2 << 30, bytes_accessed=4 << 20, transcendentals=0),
        name="rows_pair",
    )(links, own, even, other, modes, couple, solved, faces)


def columns_pair(links, own, first, last, modes, couple, solved, faces, owners, of_rows):
    return pl.pallas_call(
        columns_kernel,
        out_shape=(
            jax.ShapeDtypeStruct((FACES, NF, NF), F32),
            jax.ShapeDtypeStruct((NCG, FACES * MODES), F32),
        ),
        in_specs=[SMEM_SPEC] + [VMEM_SPEC] * 13,
        out_specs=(pl.BlockSpec(memory_space=pltpu.HBM), VMEM_SPEC),
        scratch_shapes=[
            pltpu.VMEM((2, NF, NF), F32), *pair_scratch(), pltpu.SemaphoreType.DMA((2,)),
        ],
        compiler_params=pltpu.CompilerParams(vmem_limit_bytes=24 << 20),
        cost_estimate=pl.CostEstimate(flops=3 << 30, bytes_accessed=4 << 20, transcendentals=0),
        name="columns_pair",
    )(links, own, first, last, modes, couple, solved, faces, owners, *of_rows)


def swap_rows(value, first):
    pairs = []
    for low in range(first, lax.axis_size("gx") - 1, 2):
        pairs += [(low, low + 1), (low + 1, low)]
    return lax.ppermute(value, "gx", pairs)


def swap_columns(value, step):
    rows, columns = lax.axis_size("gx"), lax.axis_size("gy")
    pairs = []
    for row in range(rows):
        first = step if row < rows // 2 else 1 - step
        for low in range(row * columns + first, (row + 1) * columns - 1, 2):
            pairs += [(low, low + 1), (low + 1, low)]
    return lax.ppermute(value, ("gx", "gy"), pairs)


def body(interior_inverse, coupling, face_matrix, face_modes, face_links, owner_map):
    inverse = interior_inverse[0, 0]
    couple = coupling[0, 0]
    faces = face_matrix[0, 0]
    modes = face_modes[0, 0]
    links = face_links[0, 0]
    owners = owner_map[0]
    couple, solved, faces, own, even, other, first, last = own_blocks(inverse, couple, faces)
    first_part = swap_columns(first, 0)
    even_part = swap_rows(even, 0)
    other_part = swap_rows(other, 1)
    last_part = swap_columns(last, 1)
    of_rows = rows_pair(links, own, even_part, other_part, modes, couple, solved, faces)
    deluxe, partial = columns_pair(
        links, own, first_part, last_part, modes, couple, solved, faces, owners, of_rows
    )
    count = lax.axis_size("gy")
    parts = partial.reshape(count, NCG // count, FACES * MODES)
    coarse = lax.all_to_all(parts, "gy", 0, 0).sum(0)
    return deluxe[None, None], coarse[None]


def solution(mesh):
    placed = (
        P("gx", "gy", None, None),
        P("gx", "gy", None, None),
        P("gx", "gy", None, None, None),
        P("gx", "gy", None, None),
        P("gx", "gy", None),
        P("gx", "gy", None),
    )
    return jax.shard_map(
        body,
        mesh=mesh,
        in_specs=placed,
        out_specs=(P("gx", "gy", None, None, None), P("gx", "gy", None)),
        check_vma=False,
    )
```

```python
import jax
import jax.numpy as jnp
from jax import lax
from jax.experimental import pallas as pl
from jax.experimental.pallas import tpu as pltpu
from jax.sharding import PartitionSpec as P


NI = 768
NF = 256
FACES = 4
MODES = 32
NCG = 256
HALF = NF // 2

F32 = jnp.float32
BF16 = jnp.bfloat16
NORTH, SOUTH, WEST, EAST = range(FACES)

SWEEP_TOL = 3e-4
RESIDUAL_TOL = 4e-10
BOUND = 2e-5
MAX_SQUARINGS = 40
MAX_SWEEPS = 12


def dot(left, right):
    return lax.dot_general(left, right, (((1,), (0,)), ((), ())), preferred_element_type=F32)


def dot_rows(left, right):
    return lax.dot_general(left, right, (((0,), (0,)), ((), ())), preferred_element_type=F32)


def split(value):
    high = value.astype(BF16)
    return high, (value - high.astype(F32)).astype(BF16)


def left_three(value):
    high, low = split(value)
    return jnp.concatenate([high, high, low], axis=1)


def right_three(value):
    high, low = split(value)
    return jnp.concatenate([high, low, high], axis=0)


def odd_at(axis):
    return lax.rem(lax.axis_index(axis), 2) == 1


def west_first():
    low = lax.axis_index("gx") < lax.axis_size("gx") // 2
    return odd_at("gy") == low


def grid_iota(rows, columns, dimension):
    return lax.broadcasted_iota(jnp.int32, (rows, columns), dimension)


def pack(block):
    first, last = block[:HALF, :HALF], block[HALF:, HALF:]
    rows, columns = grid_iota(HALF, HALF, 0), grid_iota(HALF, HALF, 1)
    diagonal = jnp.sum(jnp.where(rows == columns, last, 0.0), axis=0, keepdims=True)
    square = jnp.where(rows >= columns, first, last)
    return square, block[:HALF, HALF:], jnp.broadcast_to(diagonal, (8, HALF))


def unpack(packed):
    square, corner, diagonal = packed[:HALF], packed[HALF:NF], packed[NF : NF + 1]
    rows, columns = grid_iota(HALF, HALF, 0), grid_iota(HALF, HALF, 1)
    turned = square.T
    first = jnp.where(rows >= columns, square, turned)
    last = jnp.where(rows == columns, diagonal, jnp.where(rows < columns, square, turned))
    return first, corner, corner.T, last


def own_kernel(
    inverse_hbm, couple_hbm, faces_hbm,
    couple, solved, faces, own, send_even, send_odd, send_first, send_last,
    inverse, sems,
):
    half = 2 * NF
    third = NI // 3

    def couple_copy(first, at):
        columns = slice(first, first + half)
        return pltpu.make_async_copy(couple_hbm.at[:, columns], couple.at[:, columns], sems.at[at])

    left, right = couple_copy(half, 0), couple_copy(0, 1)
    rows = [slice(n * third, (n + 1) * third) for n in range(3)]
    blocks = [
        pltpu.make_async_copy(inverse_hbm.at[here], inverse.at[here], sems.at[2 + n])
        for n, here in enumerate(rows)
    ]
    faces_copy = pltpu.make_async_copy(faces_hbm, faces, sems.at[5])
    for copy in [left, *blocks, faces_copy, right]:
        copy.start()
    left.wait()
    for block, here in zip(blocks, rows, strict=True):
        block.wait()
        solved[here, half:] = dot(inverse[here, :], couple[:, half:]).astype(BF16)
    faces_copy.wait()

    def own_of(n):
        columns = slice(n * NF, (n + 1) * NF)
        gram = dot_rows(couple[:, columns], solved[:, columns])
        block = faces[n].astype(F32) - 0.5 * (gram + gram.T)
        own[n] = block
        return pack(block)

    def put(ref, parts):
        ref[:HALF], ref[HALF:NF], ref[NF:] = parts

    def put_pair(odd, low, high, up, down):
        pairs = list(zip(low, high, strict=True))
        put(up, [jnp.where(odd, l, h) for l, h in pairs])
        put(down, [jnp.where(odd, h, l) for l, h in pairs])

    put_pair(west_first(), own_of(WEST), own_of(EAST), send_first, send_last)
    right.wait()
    solved[:, :half] = dot(inverse[...], couple[:, :half]).astype(BF16)
    put_pair(odd_at("gx"), own_of(NORTH), own_of(SOUTH), send_even, send_odd)


def own_blocks(inverse, couple, faces):
    vmem = pl.BlockSpec(memory_space=pltpu.VMEM)
    hbm = pl.BlockSpec(memory_space=pltpu.HBM)
    send = jax.ShapeDtypeStruct((NF + 8, HALF), F32)
    return pl.pallas_call(
        own_kernel,
        out_shape=(
            jax.ShapeDtypeStruct((NI, FACES * NF), BF16),
            jax.ShapeDtypeStruct((NI, FACES * NF), BF16),
            jax.ShapeDtypeStruct((FACES, NF, NF), BF16),
            jax.ShapeDtypeStruct((FACES, NF, NF), F32),
            send, send, send, send,
        ),
        in_specs=[hbm] * 3,
        out_specs=(vmem,) * 8,
        scratch_shapes=[pltpu.VMEM((NI, NI), BF16), pltpu.SemaphoreType.DMA((6,))],
        compiler_params=pltpu.CompilerParams(vmem_limit_bytes=20 << 20),
        name="own_blocks",
    )(*(pltpu.with_memory_space_constraint(value, pltpu.HBM) for value in (inverse, couple, faces)))


def eye():
    rows = lax.broadcasted_iota(jnp.int32, (NF, NF), 0)
    columns = lax.broadcasted_iota(jnp.int32, (NF, NF), 1)
    return rows == columns


def largest(values):
    result = values[0]
    for value in values[1:]:
        result = jnp.maximum(result, value)
    return result


def total_square(value):
    rows = jnp.sum(value * value, axis=0, keepdims=True)
    return jnp.sum(rows, axis=1, keepdims=True)


def general_solve(ids, own, deluxe, matrix, scale, sweep, rest, power):
    own_norm = []
    for n in range(2):
        m, block = matrix[n], own[ids[n]]
        by = 1.0 / jnp.sum(jnp.where(eye(), m, 0.0), axis=1, keepdims=True)
        bound = jnp.max(jnp.sum(jnp.abs(m), axis=1, keepdims=True) * by)
        factor = jnp.where(bound < 1.75, 1.0, 1.0 / bound)
        scale[n] = jnp.broadcast_to(by * factor, (NF, HALF))
        rest[n] = block
        deluxe[n] = jnp.zeros((NF, NF), F32)
        own_norm.append(jnp.sum(block * block))

    def sweep_once(state):
        count, _, now = state
        for n in range(2):
            by = jnp.concatenate([scale[n]] * 2, axis=1)
            power[n] = jnp.where(eye(), 1.0, 0.0) - by * matrix[n]
            sweep[n] = by * rest[n]

        def more(inner):
            return jnp.logical_and(inner[1] > SWEEP_TOL, inner[0] < MAX_SQUARINGS)

        def squaring(inner):
            found = []
            for n in range(2):
                error = power[n]
                start = sweep[n]
                both = dot(left_three(error), right_three(jnp.concatenate([error, start], axis=1)))
                square = both[:, :NF]
                power[n] = square
                sweep[n] = start + both[:, NF:]
                found.append(jnp.sum(square * square))
            return inner[0] + 1, largest(found)

        lax.while_loop(more, squaring, (jnp.int32(0), jnp.float32(1.0)))

        ratios = []
        for n in range(2):
            start = sweep[n]
            total = deluxe[n] + (start + dot(left_three(power[n]), right_three(start)))
            deluxe[n] = total
            residual = own[ids[n]] - dot(left_three(matrix[n]), right_three(total))
            rest[n] = residual
            ratios.append(jnp.sum(residual * residual) / own_norm[n])
        return count + 1, now, largest(ratios)

    def unsolved(state):
        count, before, now = state
        return jnp.logical_and(
            jnp.logical_and(now > RESIDUAL_TOL, now < 0.25 * before), count < MAX_SWEEPS
        )

    lax.while_loop(unsolved, sweep_once, (jnp.int32(0), jnp.float32(8.0), jnp.float32(1.0)))


def face_weights(links):
    return [links[n].astype(F32) for n in range(FACES)]


def solve_pair(ids, links, own, received, modes, couple, solved, faces, deluxe, scratch):
    matrix, scale, power, sweep, rest, general, phi = scratch
    for n in range(2):
        quarters = unpack(received[n][...])
        weight = links[ids[n]].astype(F32)
        for at, quarter in enumerate(quarters):
            here = (slice((at // 2) * HALF, (at // 2 + 1) * HALF), slice((at % 2) * HALF, (at % 2 + 1) * HALF))
            matrix[(n, *here)] = own[(ids[n], *here)] + quarter * weight

    norms = [[] for _ in range(2)]
    for n in range(2):
        by = 1.0 / jnp.sum(jnp.where(eye(), matrix[n], 0.0), axis=1, keepdims=True)
        scale[n] = jnp.broadcast_to(by, (NF, HALF))
        factor = jnp.where(eye(), 0.0, -by * matrix[n])
        norms[n].append(total_square(factor))
        start = by * own[ids[n]]
        power[0, n] = factor.astype(BF16)
        both = dot(power[0, n], jnp.concatenate([power[0, n], start.astype(BF16)], axis=1))
        square = both[:, :NF]
        norms[n].append(total_square(square))
        power[1, n] = square.astype(BF16)
        sweep[n] = start + both[:, NF:]
    for n in range(2):
        start = sweep[n]
        rounded = (start + dot(power[1, n], start.astype(BF16))).astype(BF16)
        high, low = split(matrix[n])
        residual = own[ids[n]] - (dot(high, rounded) + dot(low, rounded))
        rest[n] = jnp.concatenate([scale[n]] * 2, axis=1) * residual
        rounded = rounded.astype(F32)
        norms[n].append(total_square(rounded))
        deluxe[n] = rounded
    for n in range(2):
        start = rest[n]
        sweep[n] = start + dot(power[0, n], start.astype(BF16))
    left_out = []
    for n in range(2):
        start = sweep[n]
        step = start + dot(power[1, n], start.astype(BF16))
        deluxe[n] = deluxe[n] + step
        one, two, size = (jnp.sqrt(norm) for norm in norms[n])
        rate = norms[n][1] + (one + two) * (1.0 + one) * 2.0**-8
        left_out.append(rate * jnp.sqrt(total_square(step)) / size)

    @pl.when(jnp.logical_not(jnp.max(largest(left_out)) < BOUND))
    def _():
        general_solve(ids, own, deluxe, matrix, scale, sweep, rest, general)

    face_of = grid_iota(NF, FACES * MODES, 1) // MODES
    all_phi = jnp.zeros((NF, FACES * MODES), F32)
    for n in range(2):
        mode = jnp.where(face_of == ids[n], modes[...].astype(F32), 0.0).astype(BF16)
        mapped = dot(
            jnp.concatenate(split(deluxe[n]), axis=1), jnp.concatenate([mode, mode], axis=0)
        )
        all_phi = all_phi + mapped
        phi[n * NF : (n + 1) * NF, :] = jnp.concatenate(split(mapped), axis=1)

    def times_phi(left):
        both = dot(left, phi[...])
        return both[:, : FACES * MODES] + both[:, FACES * MODES :]

    def columns_of(ref):
        return jnp.concatenate([ref[:, pl.ds(pl.multiple_of(face * NF, NF), NF)] for face in ids], axis=1)

    return (
        times_phi(columns_of(couple)),
        times_phi(columns_of(solved)),
        times_phi(jnp.concatenate([faces[face] for face in ids], axis=1)),
        all_phi,
    )


def early_faces():
    return jnp.where(west_first(), WEST, EAST), jnp.where(odd_at("gx"), NORTH, SOUTH)


def late_faces():
    return jnp.where(west_first(), EAST, WEST), jnp.where(odd_at("gx"), SOUTH, NORTH)


def early_kernel(
    links, own, first, even, modes, couple, solved, faces,
    deluxe, left, right, faces_phi, all_phi,
    *scratch,
):
    left[...], right[...], faces_phi[...], all_phi[...] = solve_pair(
        early_faces(), links, own, (first, even), modes, couple, solved, faces, deluxe, scratch
    )


def late_kernel(
    links, own, last, other, modes, couple, solved, faces, owners,
    deluxe_early, left_early, right_early, faces_phi_early, all_phi_early,
    deluxe_hbm, partial,
    deluxe, *scratch_sems,
):
    *scratch, sems = scratch_sems
    weight = face_weights(links)

    def out(source, n, ids):
        at = 2 * n if source is deluxe else 2 * n + 1
        return pltpu.make_async_copy(source.at[n], deluxe_hbm.at[ids[n]], sems.at[at])

    for n in range(2):
        out(deluxe_early, n, early_faces()).start()
    left, right, faces_phi, all_phi = solve_pair(
        late_faces(), links, own, (last, other), modes, couple, solved, faces, deluxe, scratch
    )
    for n in range(2):
        out(deluxe, n, late_faces()).start()
    cross = dot_three_rows(left + left_early[...], right + right_early[...])
    own_part = dot_three_rows(all_phi + all_phi_early[...], faces_phi + faces_phi_early[...])
    rows = grid_iota(FACES * MODES, FACES * MODES, 0)
    columns = grid_iota(FACES * MODES, FACES * MODES, 1)
    same = (rows // MODES) == (columns // MODES)
    local = jnp.where(same, own_part, 0.0) - 0.5 * (cross + cross.T)

    def spread(index):
        face = index // MODES
        value = jnp.zeros(index.shape, F32)
        for n in range(FACES):
            value = jnp.where(face == n, weight[n], value)
        return value

    local = local * spread(rows) * spread(columns)
    slots = lax.broadcasted_iota(jnp.int32, (NCG, FACES * MODES), 0)
    onehot = jnp.where(owners[...] == slots, 1.0, 0.0).astype(BF16)
    high, low = split(local)
    lowest = (local - high.astype(F32) - low.astype(F32)).astype(BF16)
    partial[...] = dot(onehot, high) + (dot(onehot, low) + dot(onehot, lowest))
    for n in range(2):
        out(deluxe_early, n, early_faces()).wait()
        out(deluxe, n, late_faces()).wait()


def dot_three_rows(one, two):
    one_high, one_low = split(one)
    two_high, two_low = split(two)
    return dot_rows(one_high, two_high) + (dot_rows(one_high, two_low) + dot_rows(one_low, two_high))


VMEM_SPEC = pl.BlockSpec(memory_space=pltpu.VMEM)
SMEM_SPEC = pl.BlockSpec(memory_space=pltpu.SMEM)


def pair_scratch():
    square = pltpu.VMEM((2, NF, NF), F32)
    return [
        square,
        pltpu.VMEM((2, NF, HALF), F32),
        pltpu.VMEM((2, 2, NF, NF), BF16),
        square,
        square,
        square,
        pltpu.VMEM((2 * NF, 2 * FACES * MODES), BF16),
    ]


def early_pair(links, own, first, even, modes, couple, solved, faces):
    tall = jax.ShapeDtypeStruct((NI, FACES * MODES), F32)
    short = jax.ShapeDtypeStruct((NF, FACES * MODES), F32)
    return pl.pallas_call(
        early_kernel,
        out_shape=(jax.ShapeDtypeStruct((2, NF, NF), F32), tall, tall, short, short),
        in_specs=[SMEM_SPEC] + [VMEM_SPEC] * 7,
        out_specs=(VMEM_SPEC,) * 5,
        scratch_shapes=pair_scratch(),
        compiler_params=pltpu.CompilerParams(vmem_limit_bytes=24 << 20),
        cost_estimate=pl.CostEstimate(flops=2 << 30, bytes_accessed=4 << 20, transcendentals=0),
        name="early_pair",
    )(links, own, first, even, modes, couple, solved, faces)


def late_pair(links, own, last, other, modes, couple, solved, faces, owners, early):
    return pl.pallas_call(
        late_kernel,
        out_shape=(
            jax.ShapeDtypeStruct((FACES, NF, NF), F32),
            jax.ShapeDtypeStruct((NCG, FACES * MODES), F32),
        ),
        in_specs=[SMEM_SPEC] + [VMEM_SPEC] * 13,
        out_specs=(pl.BlockSpec(memory_space=pltpu.HBM), VMEM_SPEC),
        scratch_shapes=[
            pltpu.VMEM((2, NF, NF), F32), *pair_scratch(), pltpu.SemaphoreType.DMA((4,)),
        ],
        compiler_params=pltpu.CompilerParams(vmem_limit_bytes=24 << 20),
        cost_estimate=pl.CostEstimate(flops=3 << 30, bytes_accessed=4 << 20, transcendentals=0),
        name="late_pair",
    )(links, own, last, other, modes, couple, solved, faces, owners, *early)


def swap_rows(value, first):
    pairs = []
    for low in range(first, lax.axis_size("gx") - 1, 2):
        pairs += [(low, low + 1), (low + 1, low)]
    return lax.ppermute(value, "gx", pairs)


def swap_columns(value, step):
    rows, columns = lax.axis_size("gx"), lax.axis_size("gy")
    pairs = []
    for row in range(rows):
        first = step if row < rows // 2 else 1 - step
        for low in range(row * columns + first, (row + 1) * columns - 1, 2):
            pairs += [(low, low + 1), (low + 1, low)]
    return lax.ppermute(value, ("gx", "gy"), pairs)


def body(interior_inverse, coupling, face_matrix, face_modes, face_links, owner_map):
    inverse = interior_inverse[0, 0]
    couple = coupling[0, 0]
    faces = face_matrix[0, 0]
    modes = face_modes[0, 0]
    links = face_links[0, 0]
    owners = owner_map[0]
    couple, solved, faces, own, even, other, first, last = own_blocks(inverse, couple, faces)
    first_part = swap_columns(first, 0)
    even_part = swap_rows(even, 0)
    other_part = swap_rows(other, 1)
    last_part = swap_columns(last, 1)
    early = early_pair(links, own, first_part, even_part, modes, couple, solved, faces)
    deluxe, partial = late_pair(
        links, own, last_part, other_part, modes, couple, solved, faces, owners, early
    )
    count = lax.axis_size("gy")
    parts = partial.reshape(count, NCG // count, FACES * MODES)
    coarse = lax.all_to_all(parts, "gy", 0, 0).sum(0)
    return deluxe[None, None], coarse[None]


def solution(mesh):
    placed = (
        P("gx", "gy", None, None),
        P("gx", "gy", None, None),
        P("gx", "gy", None, None, None),
        P("gx", "gy", None, None),
        P("gx", "gy", None),
        P("gx", "gy", None),
    )
    return jax.shard_map(
        body,
        mesh=mesh,
        in_specs=placed,
        out_specs=(P("gx", "gy", None, None, None), P("gx", "gy", None)),
        check_vma=False,
    )
```
